512 devices in a mesh: ta: 64 (over z, x, core), pa: 8 (over y).
Axes of the slice: x: 4, y: 8, z: 8, core: 2. Of those that a mesh axis runs over, the one named last changes fastest.
Arguments:
- occupied_orbitals: bfloat16 [4096, 512], P('pa'), may hold values from -3 to 3
- virtual_orbitals: bfloat16 [4096, 1536], P('pa'), may hold values from -2.5 to 2.5
- occupied_gaps: float32 [512], replicated, may hold values from 0.05 to 2
- virtual_gaps: float32 [1536], replicated, may hold values from 0.05 to 2
- tile_columns: int32 [32, 8], replicated, may hold values from 0 to 31, as said below
- probe_vectors: bfloat16 [32, 4096], P(None, 'ta'), may hold values from -0.1875 to 0.1875
Outputs:
- response: float32 [64, 32, 4096], P('ta', None, 'pa')
The draws below stay inside these ranges and needn't reach their ends.
Inputs may be any that keep to these rules, and one draw needn't show every extreme that they name: `tile_columns`: each row block lists 8 different column blocks, and every column block is listed by some row block.
All inputs are finite; a program needn't handle non-finite values.
Results may differ from the reference program's by a relative error of at most 0.00083.
Values may be sent and summed in bfloat16 or wider, within the bound.
A program may use at most 64 MiB of HBM per device.

```python
import math
import jax
import jax.numpy as jnp
from jax import lax

NPTS = 4096
NO = 512
NV = 1536
BLK = 128
KB = 8
NT = 32
NVEC = 32
NF = 64


def draw_tile_columns(key, part):
    block_total = NPTS // BLK
    first_key, second_key = jax.random.split(key)
    diagonal_order = jax.random.permutation(first_key, block_total).astype(jnp.int32)
    row_keys = jax.random.split(second_key, block_total)
    shifts = jax.vmap(lambda row_key: jax.random.permutation(row_key, block_total - 1))(row_keys)[:, :KB - 1].astype(jnp.int32)
    rows_here = jnp.arange(block_total, dtype=jnp.int32)
    others = diagonal_order[(rows_here[:, None] + 1 + shifts) % block_total]
    return jnp.concatenate([diagonal_order[:, None], others], axis=1).astype(jnp.int32)


def steps_of(stream_key, extent, cuts, low, top_value):
    def one(position, shards_of):
        draws = jax.random.uniform(jax.random.fold_in(jax.random.fold_in(stream_key, 6), position), (shards_of,), jnp.float32, low / len(cuts), top_value / len(cuts))
        return jnp.repeat(jnp.exp(draws), extent[position] // shards_of).reshape((-1,) + (1,) * (len(extent) - position - 1))

    factor_of = one(*cuts[0])
    for cut in cuts[1:]:
        factor_of = factor_of * one(*cut)
    return factor_of


def gaussian(key, dims, width, limit, cuts=(), kind=jnp.bfloat16):
    result = width * jax.random.normal(key, dims, jnp.float32)
    if cuts:
        result = result * steps_of(key, dims, cuts, -0.22, 0.18)
    return jnp.clip(result, -limit, limit).astype(kind)


def setup_inputs(seed: int = 0) -> dict:
    key_list = jax.random.split(jax.random.key(seed), 7)
    occupied_orbitals = gaussian(key_list[0], (NPTS, NO), 0.21, 3.0, ((0, 8),))
    virtual_orbitals = gaussian(key_list[1], (NPTS, NV), 0.16, 2.5, ((0, 8),))
    occupied_gaps = jnp.clip(jnp.exp(jax.random.uniform(key_list[2], (NO,), jnp.float32, math.log(0.05), math.log(2.0))), 0.05, 2.0)
    virtual_gaps = jnp.clip(jnp.exp(jax.random.uniform(key_list[3], (NV,), jnp.float32, math.log(0.05), math.log(2.0))), 0.05, 2.0)
    tile_columns = draw_tile_columns(jax.random.fold_in(key_list[6], 71), 0)
    probe_vectors = gaussian(key_list[5], (NVEC, NPTS), (KB * BLK) ** -0.5, 0.1875, ((1, 64),))
    return {"occupied_orbitals": occupied_orbitals, "virtual_orbitals": virtual_orbitals, "occupied_gaps": occupied_gaps, "virtual_gaps": virtual_gaps, "tile_columns": tile_columns, "probe_vectors": probe_vectors}


def quadrature_grids(count_times, count_freqs):
    low_time = jnp.log(jnp.float32(0.05))
    high_time = jnp.log(jnp.float32(8.0))
    time_place = (jnp.arange(count_times, dtype=jnp.float32) + 0.5) / count_times
    times_grid = jnp.exp(low_time + (high_time - low_time) * time_place)
    weights_grid = times_grid * (high_time - low_time) / count_times
    low_freq = jnp.log(jnp.float32(0.05))
    high_freq = jnp.log(jnp.float32(20.0))
    freq_place = (jnp.arange(count_freqs, dtype=jnp.float32) + 0.5) / count_freqs
    freqs_grid = jnp.exp(low_freq + (high_freq - low_freq) * freq_place)
    cosine_table = 2.0 * weights_grid[None, :] * jnp.cos(freqs_grid[:, None] * times_grid[None, :])
    return times_grid, cosine_table


def reference(occupied_orbitals, virtual_orbitals, occupied_gaps, virtual_gaps, tile_columns, probe_vectors):
    times_grid, cosine_table = quadrature_grids(NT, NF)
    occ_weights = jnp.exp(-times_grid[:, None] * occupied_gaps[None, :])
    virt_weights = jnp.exp(-times_grid[:, None] * virtual_gaps[None, :])
    highest = lax.Precision.HIGHEST

    def row_block(block_index):
        row_occ = lax.dynamic_slice_in_dim(occupied_orbitals, block_index * BLK, BLK, 0).astype(jnp.float32)
        row_virt = lax.dynamic_slice_in_dim(virtual_orbitals, block_index * BLK, BLK, 0).astype(jnp.float32)

        def one_tile(column_block):
            first_point = column_block * BLK
            col_occ = lax.dynamic_slice_in_dim(occupied_orbitals, first_point, BLK, 0).astype(jnp.float32)
            col_virt = lax.dynamic_slice_in_dim(virtual_orbitals, first_point, BLK, 0).astype(jnp.float32)
            scaled_occ = lax.optimization_barrier((col_occ[None] * occ_weights[:, None, :]).astype(jnp.bfloat16)).astype(jnp.float32)
            scaled_virt = lax.optimization_barrier((col_virt[None] * virt_weights[:, None, :]).astype(jnp.bfloat16)).astype(jnp.float32)
            green_occ = jnp.einsum('tci,ri->tcr', scaled_occ, row_occ, precision=highest)
            green_virt = jnp.einsum('tca,ra->tcr', scaled_virt, row_virt, precision=highest)
            polar = lax.optimization_barrier((green_occ * green_virt).astype(jnp.bfloat16)).astype(jnp.float32)
            col_vectors = lax.dynamic_slice_in_dim(probe_vectors, first_point, BLK, 1).astype(jnp.float32)
            return jnp.einsum('vc,tcr->tvr', col_vectors, polar, precision=highest)

        tile_terms = lax.map(one_tile, tile_columns[block_index].astype(jnp.int32))
        return jnp.sum(tile_terms, axis=0)

    block_total = NPTS // BLK
    block_terms = lax.map(row_block, jnp.arange(block_total).astype(jnp.int32))
    time_terms = jnp.transpose(block_terms, (1, 2, 0, 3)).reshape(NT, NVEC, NPTS)
    return jnp.einsum('kt,tvr->kvr', cosine_table, time_terms, precision=highest)
```

```python
import functools

import jax
import jax.numpy as jnp
import numpy as np
from jax import lax
from jax.experimental import pallas as pl
from jax.experimental.pallas import tpu as pltpu
from jax.sharding import PartitionSpec as P

MESH = pl.DeviceIdType.MESH
NT = 32
NVEC = 32
BLK = 128
NZ = 8
NX = 4
NY = 8
COLS = 16
CHIP_COLS = NY * COLS
ROWS = 256
LINK = jnp.bfloat16


def quadrature_grids(count_times, count_freqs):
    place = (np.arange(count_times) + 0.5) / count_times
    times = np.exp(np.log(0.05) + np.log(160.0) * place)
    freqs = np.exp(np.log(0.05) + np.log(400.0) * (np.arange(count_freqs) + 0.5) / count_freqs)
    table = 2.0 * times[None, :] * np.log(160.0) / count_times * np.cos(freqs[:, None] * times[None, :])
    return times.astype(np.float32), table.astype(np.float32)


def owner_block(x):
    high = jnp.where((x == 1) | (x == 2), 1, 0)
    low = jnp.where(x >= 2, 1, 0)
    return 2 * high + low


def kernel(
    occ_hbm, virt_hbm, ogap_ref, vgap_ref, tiles_ref, probe_ref, times_ref, table_ref, out_ref,
    points, r_occ, r_virt, weights, s_occ, s_virt, polar, padded, probes, picked_out, picked_in, left,
    keep, x1_out, x1_in, x2_out, x2_in, sums, zs_out, zs_in, trans, za_in, xa_out, whole,
    local_sem, y_send, y_recv, f_send, f_recv, p_send, p_recv, ps_send, ps_recv,
    x_send, x_recv, zs_send, zs_recv, za_send, za_recv, xa_send, xa_recv,
):
    ta = lax.axis_index("ta")
    y = lax.axis_index("pa")
    z = ta // 8
    e = ta % 8
    x = e // 2
    c = e % 2
    n_occ = occ_hbm.shape[1]
    n_virt = virt_hbm.shape[1]
    h_occ, h_virt = n_occ // 2, n_virt // 2

    def at(z_, e_, y_):
        return (z_ * 8 + e_, y_)

    barrier = pltpu.get_barrier_semaphore()
    for d in range(1, 8):
        for who in (at(lax.rem(z + d, NZ), e, y), at(z, lax.rem(e + d, 8), y)):
            pl.semaphore_signal(barrier, inc=1, device_id=who, device_id_type=MESH)
    for d in (1, 2, 6, 7):
        pl.semaphore_signal(
            barrier, inc=1, device_id=at(z, e, lax.rem(y + d, NY)), device_id_type=MESH
        )

    first = pl.multiple_of(x * 128 + z * COLS, COLS)
    mine = pl.ds(first, COLS)
    row0 = pl.multiple_of(c * ROWS, ROWS)
    own_copies = []
    for h in range(2):
        own_copies += [
            pltpu.make_async_copy(
                occ_hbm.at[mine, h * h_occ:(h + 1) * h_occ], points.at[0, h, :, :h_occ],
                local_sem.at[h]),
            pltpu.make_async_copy(
                virt_hbm.at[mine, h * h_virt:(h + 1) * h_virt], points.at[0, h, :, h_occ:],
                local_sem.at[2 + h]),
        ]
    row_copies = [
        pltpu.make_async_copy(occ_hbm.at[pl.ds(row0, ROWS), :], r_occ, local_sem.at[4]),
        pltpu.make_async_copy(virt_hbm.at[pl.ds(row0, ROWS), :], r_virt, local_sem.at[5]),
    ]
    for copy in own_copies + row_copies:
        copy.start()
    padded[:, :64] = probe_ref[...]
    padded[:, 64:] = jnp.zeros((NVEC, 64), jnp.bfloat16)
    for copy in own_copies:
        copy.wait()
    pl.semaphore_wait(barrier, 18)

    sends = []

    def remote(src, dst, send, recv, who):
        copy = pltpu.make_async_remote_copy(
            src_ref=src, dst_ref=dst, send_sem=send, recv_sem=recv, device_id=who,
            device_id_type=MESH,
        )
        copy.start()
        sends.append(copy)
        return copy

    def along_y(source, target, step, sem, part=slice(None)):
        return remote(
            points.at[source, c, :, part], points.at[target, c, :, part], y_send.at[sem],
            y_recv.at[sem], at(z, e, lax.rem(y + step + NY, NY)),
        )

    gathers = {
        2: along_y(0, 2, -2, 2), 6: along_y(0, 6, 2, 6), 1: along_y(0, 1, -1, 1),
        7: along_y(0, 7, 1, 7),
    }
    sibling = at(z, x * 2 + 1 - c, y)
    probe_copies = []
    for d in range(1, 8):
        probe_copies.append(
            remote(padded, probes.at[z], p_send.at[d], p_recv.at[d],
                   at(lax.rem(z + d, NZ), e, y))
        )
    probes[z] = padded[...]

    weights[:, :n_occ] = jnp.exp(-times_ref[...] * ogap_ref[...])
    for j in range(n_virt // 128):
        weights[:, n_occ + j * 128:n_occ + (j + 1) * 128] = jnp.exp(
            -times_ref[...] * vgap_ref[j:j + 1, :]
        )

    tiles = tiles_ref[...]
    lane32 = lax.broadcasted_iota(jnp.int32, (1, 32), 1)
    lane_r = lax.broadcasted_iota(jnp.int32, (1, ROWS), 1)
    row_block = y * 4 + c * 2
    for copy in row_copies:
        copy.wait()

    def chunk(d, t_half):
        column_block = lax.rem(y + d, NY) * 4 + x
        hit = jnp.max(jnp.where(tiles == column_block, 1.0, 0.0), axis=0, keepdims=True)
        first_hit = jnp.sum(jnp.where(lane32 == row_block, hit, 0.0), axis=1, keepdims=True)
        second_hit = jnp.sum(jnp.where(lane32 == row_block + 1, hit, 0.0), axis=1, keepdims=True)
        mask = jnp.where(lane_r < BLK, first_hit, second_hit)
        for h in range(2):
            xo = points[d, h, :, :h_occ].astype(jnp.float32)
            xv = points[d, h, :, h_occ:].astype(jnp.float32)
            occ_lanes = slice(h * h_occ, (h + 1) * h_occ)
            virt_lanes = slice(h * h_virt, (h + 1) * h_virt)
            for t in range(16):
                row = t_half * 16 + t
                s_occ[t_half, t * COLS:(t + 1) * COLS, occ_lanes] = (
                    xo * weights[row:row + 1, occ_lanes]
                ).astype(jnp.bfloat16)
                s_virt[t_half, t * COLS:(t + 1) * COLS, virt_lanes] = (
                    xv * weights[row:row + 1, n_occ + h * h_virt:n_occ + (h + 1) * h_virt]
                ).astype(jnp.bfloat16)
        dims = (((1,), (1,)), ((), ()))
        green_occ = lax.dot_general(
            s_occ[t_half], r_occ[...], dims, preferred_element_type=jnp.float32
        )
        green_virt = lax.dot_general(
            s_virt[t_half], r_virt[...], dims, preferred_element_type=jnp.float32
        )
        value = (green_occ * green_virt * mask).astype(jnp.bfloat16)
        polar[t_half * 16:(t_half + 1) * 16, d * COLS:(d + 1) * COLS, :] = value.reshape(
            16, COLS, ROWS
        )

    siblings = {}

    def forward(d):
        siblings[d] = remote(
            points.at[d, c], points.at[d, c], f_send.at[d], f_recv.at[d], sibling
        )

    def both(d):
        siblings[d].wait_recv()
        chunk(d, 0)
        chunk(d, 1)

    chunk(0, 0)
    chunk(0, 1)
    quarter = (h_occ + h_virt) // 2
    gathers[2].wait_recv()
    gathers[3] = along_y(2, 3, -1, 3)
    gathers[4] = along_y(2, 4, -2, 4, slice(0, quarter))
    gathers[6].wait_recv()
    gathers[5] = along_y(6, 5, 1, 5)
    gathers[8] = along_y(6, 4, 2, 8, slice(quarter, 2 * quarter))
    for d in (2, 6):
        forward(d)
    for d in (1, 7):
        gathers[d].wait_recv()
        forward(d)
    both(1)
    both(7)
    for d in (3, 5):
        gathers[d].wait_recv()
        forward(d)
    both(2)
    both(6)
    gathers[4].wait_recv()
    gathers[8].wait_recv()
    forward(4)

    for copy in probe_copies:
        copy.wait_recv()
    lane = lax.broadcasted_iota(jnp.int32, (128, CHIP_COLS), 1)
    source = lax.broadcasted_iota(jnp.int32, (128, CHIP_COLS), 0)
    matched = source == lax.rem(z, 4) * COLS + lane % COLS
    gathered = jnp.zeros((NVEC, CHIP_COLS), jnp.float32)
    for q in range(NY):
        slot = lax.rem(q - y + NY, NY)
        pick = jnp.where((lane // COLS == slot) & matched, 1.0, 0.0).astype(jnp.bfloat16)
        gathered += jnp.dot(probes[q], pick, preferred_element_type=jnp.float32)
    picked_out[...] = gathered.astype(jnp.bfloat16)
    probe_forward = remote(picked_out, picked_in, ps_send, ps_recv, sibling)
    both(3)
    both(5)
    probe_forward.wait_recv()
    gathered = jnp.where(
        z // 4 == c, picked_out[...].astype(jnp.float32), picked_in[...].astype(jnp.float32)
    )
    gathered = gathered.astype(jnp.bfloat16)
    near, far = x + 1 - 2 * lax.rem(x, 2), 3 - x
    orders = (
        (owner_block(3 - near), owner_block(near), owner_block(far), owner_block(x)),
        (owner_block(far + 1 - 2 * lax.rem(far, 2)), owner_block(far), owner_block(near),
         owner_block(x)),
    )
    to_row = lax.broadcasted_iota(jnp.int32, (NVEC, NVEC), 0)
    from_row = lax.broadcasted_iota(jnp.int32, (NVEC, NVEC), 1)
    for half, blocks in enumerate(orders):
        block = jnp.where(
            to_row < 16,
            jnp.where(to_row < 8, blocks[0], blocks[1]),
            jnp.where(to_row < 24, blocks[2], blocks[3]),
        )
        order = jnp.where(from_row == block * 8 + to_row % 8, 1.0, 0.0).astype(jnp.bfloat16)
        left[half] = jnp.dot(order, gathered, preferred_element_type=jnp.float32).astype(
            jnp.bfloat16
        )

    partners = (at(z, near * 2 + c, y), at(z, far * 2 + c, y))
    exchanges = []
    siblings[4].wait_recv()
    for half in range(2):
        chunk(4, half)
        for t in range(16):
            terms = jnp.dot(
                left[half], polar[half * 16 + t], preferred_element_type=jnp.float32
            )
            x1_out[half, t * 16:(t + 1) * 16, :] = terms[:16].astype(LINK)
            keep[half, t] = terms[16:]
        exchanges.append(
            remote(x1_out.at[half], x1_in.at[half], x_send.at[half], x_recv.at[half],
                   partners[half])
        )
    seconds = []
    for half in range(2):
        exchanges[half].wait_recv()
        for t in range(16):
            total = keep[half, t] + x1_in[half, t * 16:(t + 1) * 16, :].astype(jnp.float32)
            x2_out[half, t * 8:(t + 1) * 8, :] = total[:8].astype(LINK)
            for side in range(2):
                sums[side, (half * 16 + t) * 8:(half * 16 + t + 1) * 8, :] = total[
                    8:, side * 128:(side + 1) * 128
                ]
        seconds.append(
            remote(x2_out.at[half], x2_in.at[half], x_send.at[2 + half], x_recv.at[2 + half],
                   partners[1 - half])
        )
    for half in range(2):
        seconds[half].wait_recv()
        part = slice(half * 128, (half + 1) * 128)
        arrived = x2_in[half].astype(jnp.float32)
        for side in range(2):
            sums[side, part, :] += arrived[:, side * 128:(side + 1) * 128]

    for s in range(NZ):
        for side in range(2):
            picked = sums[side, pl.ds(s, NT, stride=8), :]
            zs_out[s, :, side * 128:(side + 1) * 128] = picked
    reduces = []
    for d in (4, 3, 5, 2, 6, 1, 7):
        to = lax.rem(z + d, NZ)
        reduces.append(
            remote(zs_out.at[to], zs_in.at[d], zs_send.at[d], zs_recv.at[d], at(to, e, y))
        )
    total = zs_out[z]
    for copy, d in reversed(list(zip(reduces, (4, 3, 5, 2, 6, 1, 7)))):
        copy.wait_recv()
        total += zs_in[d]

    result = jnp.dot(
        table_ref[...], total, preferred_element_type=jnp.float32,
        precision=lax.Precision.HIGHEST,
    )
    for side in range(2):
        trans[:, side] = result[:, side * 128:(side + 1) * 128].reshape(NZ, 8, 128)
    slot = pl.ds(pl.multiple_of(z * 8, 8), 8)
    moves = []
    for d in (4, 3, 5, 2, 6, 1, 7):
        to = lax.rem(z + d, NZ)
        moves.append(
            remote(trans.at[to], za_in.at[:, slot, :], za_send.at[d], za_recv.at[d],
                   at(to, e, y))
        )
    za_in[:, slot, :] = trans[z]
    for copy in moves:
        copy.wait_recv()
    for k in range(8):
        for side in range(2):
            xa_out[k, :, side * 128:(side + 1) * 128] = za_in[side, pl.ds(k, 8, stride=8), :]
    place = (
        pl.ds(pl.multiple_of(owner_block(x) * 8, 8), 8),
        pl.ds(pl.multiple_of(c * ROWS, ROWS), ROWS),
    )
    finals = []
    for d in (4, 3, 5, 2, 6, 1, 7):
        to = lax.rem(e + d, 8)
        finals.append(
            remote(xa_out.at[to], whole.at[place], xa_send.at[d], xa_recv.at[d], at(z, to, y))
        )
    whole[place] = xa_out[e]
    for copy in finals:
        copy.wait_recv()
    out_ref[0] = whole[...]
    for copy in sends:
        copy.wait_send()


def shards(occ, virt, ogap, vgap, tiles, probe):
    times, table = quadrature_grids(NT, 64)
    n_occ, n_virt = occ.shape[1], virt.shape[1]
    n_all = n_occ + n_virt
    bf16, f32 = jnp.bfloat16, jnp.float32
    dma = pltpu.SemaphoreType.DMA
    vmem = pl.BlockSpec(memory_space=pltpu.VMEM)
    hbm = pl.BlockSpec(memory_space=pl.ANY)
    return pl.pallas_call(
        kernel,
        out_shape=jax.ShapeDtypeStruct((1, NVEC, occ.shape[0]), f32),
        in_specs=[hbm, hbm, vmem, vmem, vmem, vmem, vmem, vmem],
        out_specs=vmem,
        scratch_shapes=[
            pltpu.VMEM((NY, 2, COLS, n_all // 2), bf16),
            pltpu.VMEM((ROWS, n_occ), bf16),
            pltpu.VMEM((ROWS, n_virt), bf16),
            pltpu.VMEM((NT, n_all), f32),
            pltpu.VMEM((2, 16 * COLS, n_occ), bf16),
            pltpu.VMEM((2, 16 * COLS, n_virt), bf16),
            pltpu.VMEM((NT, CHIP_COLS, ROWS), bf16),
            pltpu.VMEM((NVEC, 128), bf16),
            pltpu.VMEM((NZ, NVEC, 128), bf16),
            pltpu.VMEM((NVEC, CHIP_COLS), bf16),
            pltpu.VMEM((NVEC, CHIP_COLS), bf16),
            pltpu.VMEM((2, NVEC, CHIP_COLS), bf16),
            pltpu.VMEM((2, 16, 16, ROWS), f32),
            pltpu.VMEM((2, 256, ROWS), LINK),
            pltpu.VMEM((2, 256, ROWS), LINK),
            pltpu.VMEM((2, 128, ROWS), LINK),
            pltpu.VMEM((2, 128, ROWS), LINK),
            pltpu.VMEM((2, NT * 8, 128), f32),
            pltpu.VMEM((NZ, NT, ROWS), f32),
            pltpu.VMEM((NZ, NT, ROWS), f32),
            pltpu.VMEM((NZ, 2, 8, 128), f32),
            pltpu.VMEM((2, NZ * 8, 128), f32),
            pltpu.VMEM((8, 8, ROWS), f32),
            pltpu.VMEM((NVEC, 2 * ROWS), f32),
            dma((6,)),
            dma((9,)), dma((9,)), dma((8,)), dma((8,)),
            dma((8,)), dma((8,)), dma, dma,
            dma((4,)), dma((4,)),
            dma((8,)), dma((8,)), dma((8,)), dma((8,)), dma((8,)), dma((8,)),
        ],
        compiler_params=pltpu.CompilerParams(collective_id=0, has_side_effects=True),
    )(
        occ, virt, ogap.reshape(1, -1), vgap.reshape(-1, 128), tiles.T, probe,
        jnp.asarray(times).reshape(NT, 1), jnp.asarray(table),
    )


def solution(mesh):
    placed = (P("pa", None), P("pa", None), P(), P(), P(), P(None, "ta"))
    return jax.shard_map(
        shards, mesh=mesh, in_specs=placed, out_specs=P("ta", None, "pa"), check_vma=False
    )
```

```python
import functools

import jax
import jax.numpy as jnp
import numpy as np
from jax import lax
from jax.experimental import pallas as pl
from jax.experimental.pallas import tpu as pltpu
from jax.sharding import PartitionSpec as P

MESH = pl.DeviceIdType.MESH
NT = 32
NVEC = 32
NF = 64
BLK = 128
NZ = 8
NX = 4
NY = 8
COLS = 16
CHIP_COLS = NY * COLS
ROWS = 256
LINK = jnp.bfloat16


def quadrature_grids(count_times, count_freqs):
    place = (np.arange(count_times) + 0.5) / count_times
    times = np.exp(np.log(0.05) + np.log(160.0) * place)
    freqs = np.exp(np.log(0.05) + np.log(400.0) * (np.arange(count_freqs) + 0.5) / count_freqs)
    table = 2.0 * times[None, :] * np.log(160.0) / count_times * np.cos(freqs[:, None] * times[None, :])
    return times.astype(np.float32), table.astype(np.float32)


def owner_block(x):
    high = jnp.where((x == 1) | (x == 2), 1, 0)
    low = jnp.where(x >= 2, 1, 0)
    return 2 * high + low


def kernel(
    occ_hbm, virt_hbm, ogap_ref, vgap_ref, tiles_ref, probe_ref, times_ref, table_ref, out_ref,
    points, r_occ, r_virt, weights, s_occ, s_virt, polar, padded, probes, picked_out, picked_in, left,
    keep, x1_out, x1_in, x2_out, x2_in, sums, zs_out, zs_in, zs_sum, trans, arrivals,
    local_sem, y_send, y_recv, f_send, f_recv, p_send, p_recv, ps_send, ps_recv,
    x_send, x_recv, zs_send, zs_recv, out_send, out_recv,
):
    ta = lax.axis_index("ta")
    y = lax.axis_index("pa")
    z = ta // 8
    e = ta % 8
    x = e // 2
    c = e % 2
    n_occ = occ_hbm.shape[1]
    n_virt = virt_hbm.shape[1]
    h_occ, h_virt = n_occ // 2, n_virt // 2

    def at(z_, e_, y_):
        return (z_ * 8 + e_, y_)

    barrier = pltpu.get_barrier_semaphore()
    near, far = x + 1 - 2 * lax.rem(x, 2), 3 - x
    sibling = at(z, x * 2 + 1 - c, y)
    partners = (at(z, near * 2 + c, y), at(z, far * 2 + c, y))
    greeted = [sibling, *partners]
    greeted += [at(z, e, lax.rem(y + d, NY)) for d in (1, 2, 6, 7)]
    greeted += [at(lax.rem(z + d, NZ), e, y) for d in range(1, NZ)]
    for who in greeted:
        pl.semaphore_signal(barrier, inc=1, device_id=who, device_id_type=MESH)

    first = pl.multiple_of(x * 128 + z * COLS, COLS)
    mine = pl.ds(first, COLS)
    row0 = pl.multiple_of(c * ROWS, ROWS)
    own_copies = []
    for h in range(2):
        own_copies += [
            pltpu.make_async_copy(
                occ_hbm.at[mine, h * h_occ:(h + 1) * h_occ], points.at[0, h, :, :h_occ],
                local_sem.at[h]),
            pltpu.make_async_copy(
                virt_hbm.at[mine, h * h_virt:(h + 1) * h_virt], points.at[0, h, :, h_occ:],
                local_sem.at[2 + h]),
        ]
    row_copies = [
        pltpu.make_async_copy(occ_hbm.at[pl.ds(row0, ROWS), :], r_occ, local_sem.at[4]),
        pltpu.make_async_copy(virt_hbm.at[pl.ds(row0, ROWS), :], r_virt, local_sem.at[5]),
    ]
    for copy in own_copies + row_copies:
        copy.start()
    padded[:, :64] = probe_ref[...]
    padded[:, 64:] = jnp.zeros((NVEC, 64), jnp.bfloat16)
    for copy in own_copies:
        copy.wait()
    pl.semaphore_wait(barrier, len(greeted))

    sends = []

    def remote(src, dst, send, recv, who):
        copy = pltpu.make_async_remote_copy(
            src_ref=src, dst_ref=dst, send_sem=send, recv_sem=recv, device_id=who,
            device_id_type=MESH,
        )
        copy.start()
        sends.append(copy)
        return copy

    def along_y(source, target, step, sem, part=slice(None)):
        return remote(
            points.at[source, c, :, part], points.at[target, c, :, part], y_send.at[sem],
            y_recv.at[sem], at(z, e, lax.rem(y + step + NY, NY)),
        )

    gathers = {
        2: along_y(0, 2, -2, 2), 6: along_y(0, 6, 2, 6), 1: along_y(0, 1, -1, 1),
        7: along_y(0, 7, 1, 7),
    }
    probe_copies = []
    for d in range(1, 8):
        probe_copies.append(
            remote(padded, probes.at[z], p_send.at[d], p_recv.at[d],
                   at(lax.rem(z + d, NZ), e, y))
        )
    probes[z] = padded[...]

    weights[:, :n_occ] = jnp.exp(-times_ref[...] * ogap_ref[...])
    for j in range(n_virt // 128):
        weights[:, n_occ + j * 128:n_occ + (j + 1) * 128] = jnp.exp(
            -times_ref[...] * vgap_ref[j:j + 1, :]
        )

    tiles = tiles_ref[...]
    lane32 = lax.broadcasted_iota(jnp.int32, (1, 32), 1)
    lane_r = lax.broadcasted_iota(jnp.int32, (1, ROWS), 1)
    row_block = y * 4 + c * 2
    for copy in row_copies:
        copy.wait()

    def chunk(d, t_half):
        column_block = lax.rem(y + d, NY) * 4 + x
        hit = jnp.max(jnp.where(tiles == column_block, 1.0, 0.0), axis=0, keepdims=True)
        first_hit = jnp.sum(jnp.where(lane32 == row_block, hit, 0.0), axis=1, keepdims=True)
        second_hit = jnp.sum(jnp.where(lane32 == row_block + 1, hit, 0.0), axis=1, keepdims=True)
        mask = jnp.where(lane_r < BLK, first_hit, second_hit)
        for h in range(2):
            xo = points[d, h, :, :h_occ].astype(jnp.float32)
            xv = points[d, h, :, h_occ:].astype(jnp.float32)
            occ_lanes = slice(h * h_occ, (h + 1) * h_occ)
            virt_lanes = slice(h * h_virt, (h + 1) * h_virt)
            for t in range(16):
                row = t_half * 16 + t
                s_occ[t_half, t * COLS:(t + 1) * COLS, occ_lanes] = (
                    xo * weights[row:row + 1, occ_lanes]
                ).astype(jnp.bfloat16)
                s_virt[t_half, t * COLS:(t + 1) * COLS, virt_lanes] = (
                    xv * weights[row:row + 1, n_occ + h * h_virt:n_occ + (h + 1) * h_virt]
                ).astype(jnp.bfloat16)
        dims = (((1,), (1,)), ((), ()))
        green_occ = lax.dot_general(
            s_occ[t_half], r_occ[...], dims, preferred_element_type=jnp.float32
        )
        green_virt = lax.dot_general(
            s_virt[t_half], r_virt[...], dims, preferred_element_type=jnp.float32
        )
        value = (green_occ * green_virt * mask).astype(jnp.bfloat16)
        polar[t_half * 16:(t_half + 1) * 16, d * COLS:(d + 1) * COLS, :] = value.reshape(
            16, COLS, ROWS
        )

    siblings = {}

    def forward(d):
        siblings[d] = remote(
            points.at[d, c], points.at[d, c], f_send.at[d], f_recv.at[d], sibling
        )

    def both(d):
        siblings[d].wait_recv()
        chunk(d, 0)
        chunk(d, 1)

    chunk(0, 0)
    chunk(0, 1)
    quarter = (h_occ + h_virt) // 2
    gathers[2].wait_recv()
    gathers[3] = along_y(2, 3, -1, 3)
    gathers[4] = along_y(2, 4, -2, 4, slice(0, quarter))
    gathers[6].wait_recv()
    gathers[5] = along_y(6, 5, 1, 5)
    gathers[8] = along_y(6, 4, 2, 8, slice(quarter, 2 * quarter))
    for d in (2, 6):
        forward(d)
    for d in (1, 7):
        gathers[d].wait_recv()
        forward(d)
    both(1)
    for d in (3, 5):
        gathers[d].wait_recv()
        forward(d)
    both(7)
    both(2)
    gathers[4].wait_recv()
    gathers[8].wait_recv()
    forward(4)

    for copy in probe_copies:
        copy.wait_recv()
    lane = lax.broadcasted_iota(jnp.int32, (128, CHIP_COLS), 1)
    source = lax.broadcasted_iota(jnp.int32, (128, CHIP_COLS), 0)
    matched = source == lax.rem(z, 4) * COLS + lane % COLS
    gathered = jnp.zeros((NVEC, CHIP_COLS), jnp.float32)
    for q in range(NY):
        slot = lax.rem(q - y + NY, NY)
        pick = jnp.where((lane // COLS == slot) & matched, 1.0, 0.0).astype(jnp.bfloat16)
        gathered += jnp.dot(probes[q], pick, preferred_element_type=jnp.float32)
    picked_out[...] = gathered.astype(jnp.bfloat16)
    probe_forward = remote(picked_out, picked_in, ps_send, ps_recv, sibling)
    both(6)
    both(3)
    both(5)
    probe_forward.wait_recv()
    gathered = jnp.where(
        z // 4 == c, picked_out[...].astype(jnp.float32), picked_in[...].astype(jnp.float32)
    )
    gathered = gathered.astype(jnp.bfloat16)
    orders = (
        (owner_block(3 - near), owner_block(near), owner_block(far), owner_block(x)),
        (owner_block(far + 1 - 2 * lax.rem(far, 2)), owner_block(far), owner_block(near),
         owner_block(x)),
    )
    to_row = lax.broadcasted_iota(jnp.int32, (NVEC, NVEC), 0)
    from_row = lax.broadcasted_iota(jnp.int32, (NVEC, NVEC), 1)
    for half, blocks in enumerate(orders):
        block = jnp.where(
            to_row < 16,
            jnp.where(to_row < 8, blocks[0], blocks[1]),
            jnp.where(to_row < 24, blocks[2], blocks[3]),
        )
        order = jnp.where(from_row == block * 8 + to_row % 8, 1.0, 0.0).astype(jnp.bfloat16)
        left[half] = jnp.dot(order, gathered, preferred_element_type=jnp.float32).astype(
            jnp.bfloat16
        )

    exchanges = []
    siblings[4].wait_recv()
    for half in range(2):
        chunk(4, half)
        for t in range(16):
            terms = jnp.dot(
                left[half], polar[half * 16 + t], preferred_element_type=jnp.float32
            )
            x1_out[half, t * 16:(t + 1) * 16, :] = terms[:16].astype(LINK)
            keep[half, t] = terms[16:]
        exchanges.append(
            remote(x1_out.at[half], x1_in.at[half], x_send.at[half], x_recv.at[half],
                   partners[half])
        )
    seconds = []
    for half in range(2):
        exchanges[half].wait_recv()
        for t in range(16):
            total = keep[half, t] + x1_in[half, t * 16:(t + 1) * 16, :].astype(jnp.float32)
            x2_out[half, t * 8:(t + 1) * 8, :] = total[:8].astype(LINK)
            for side in range(2):
                sums[side, half, t * 8:(t + 1) * 8, :] = total[8:, side * 128:(side + 1) * 128]
        seconds.append(
            remote(x2_out.at[half], x2_in.at[half], x_send.at[2 + half], x_recv.at[2 + half],
                   partners[1 - half])
        )

    def along_z(half, source, target, step, sem):
        return remote(source, target, zs_send.at[half, sem], zs_recv.at[half, sem],
                      at(lax.rem(z + step + NZ, NZ), e, y))

    reduces, relays = [{}, {}], []
    for half, sign in enumerate((1, -1)):
        seconds[half].wait_recv()
        arrived = x2_in[half].astype(jnp.float32)
        for side in range(2):
            lanes = slice(side * 128, (side + 1) * 128)
            sums[side, half] += arrived[:, lanes]
            for s in range(NZ):
                zs_out[half, s, :, lanes] = sums[side, half, pl.ds(s, 16, stride=8), :]
        relays.append(
            along_z(half, zs_out.at[half, lax.rem(z + 4, NZ)], zs_in.at[half, 4], sign, 4)
        )
        for d in (5, 2, 6, 1, 7):
            reduces[half][d] = along_z(
                half, zs_out.at[half, lax.rem(z + sign * d + NZ, NZ)], zs_in.at[half, d],
                sign * d, d,
            )
    for half, sign in enumerate((1, -1)):
        relays[half].wait_recv()
        zs_sum[half] = zs_in[half, 4] + zs_out[half, lax.rem(z + sign * 3 + NZ, NZ)]
        reduces[half][3] = along_z(half, zs_sum.at[half], zs_in.at[half, 3], sign * 3, 3)
    totals = []
    for half in range(2):
        total = zs_out[half, z]
        for d in (7, 1, 6, 2, 5, 3):
            reduces[half][d].wait_recv()
            total += zs_in[half, d]
        totals.append(total)

    result = jnp.dot(
        table_ref[...], jnp.concatenate(totals, axis=0), preferred_element_type=jnp.float32,
        precision=lax.Precision.HIGHEST,
    )
    for side in range(2):
        trans[:, side, :] = result[:, side * 128:(side + 1) * 128]

    def hand_out(step, carry):
        to = lax.rem(ta + step, NF)
        pltpu.make_async_remote_copy(
            src_ref=trans.at[to], dst_ref=arrivals.at[ta], send_sem=out_send, recv_sem=out_recv,
            device_id=(to, y), device_id_type=MESH,
        ).start()
        return carry

    lax.fori_loop(1, NF, hand_out, 0)
    arrivals[ta] = trans[ta]
    everything = pltpu.make_async_remote_copy(
        src_ref=trans.at[0:NF - 1], dst_ref=arrivals.at[0:NF - 1], send_sem=out_send,
        recv_sem=out_recv, device_id=sibling, device_id_type=MESH,
    )
    everything.wait_recv()
    for x_from in range(NX):
        block = (0, 2, 3, 1)[x_from]
        for c_from in range(2):
            for side in range(2):
                lanes = slice(c_from * ROWS + side * 128, c_from * ROWS + (side + 1) * 128)
                for z_from in range(NZ):
                    out_ref[0, block * 8 + z_from, lanes] = arrivals[
                        z_from * 8 + x_from * 2 + c_from, side
                    ]
    everything.wait_send()
    for copy in sends:
        copy.wait_send()


def shards(occ, virt, ogap, vgap, tiles, probe):
    times, table = quadrature_grids(NT, NF)
    n_occ, n_virt = occ.shape[1], virt.shape[1]
    n_all = n_occ + n_virt
    bf16, f32 = jnp.bfloat16, jnp.float32
    dma = pltpu.SemaphoreType.DMA
    vmem = pl.BlockSpec(memory_space=pltpu.VMEM)
    hbm = pl.BlockSpec(memory_space=pl.ANY)
    return pl.pallas_call(
        kernel,
        out_shape=jax.ShapeDtypeStruct((1, NVEC, occ.shape[0]), f32),
        in_specs=[hbm, hbm, vmem, vmem, vmem, vmem, vmem, vmem],
        out_specs=vmem,
        scratch_shapes=[
            pltpu.VMEM((NY, 2, COLS, n_all // 2), bf16),
            pltpu.VMEM((ROWS, n_occ), bf16),
            pltpu.VMEM((ROWS, n_virt), bf16),
            pltpu.VMEM((NT, n_all), f32),
            pltpu.VMEM((2, 16 * COLS, n_occ), bf16),
            pltpu.VMEM((2, 16 * COLS, n_virt), bf16),
            pltpu.VMEM((NT, CHIP_COLS, ROWS), bf16),
            pltpu.VMEM((NVEC, 128), bf16),
            pltpu.VMEM((NZ, NVEC, 128), bf16),
            pltpu.VMEM((NVEC, CHIP_COLS), bf16),
            pltpu.VMEM((NVEC, CHIP_COLS), bf16),
            pltpu.VMEM((2, NVEC, CHIP_COLS), bf16),
            pltpu.VMEM((2, 16, 16, ROWS), f32),
            pltpu.VMEM((2, 256, ROWS), LINK),
            pltpu.VMEM((2, 256, ROWS), LINK),
            pltpu.VMEM((2, 128, ROWS), LINK),
            pltpu.VMEM((2, 128, ROWS), LINK),
            pltpu.VMEM((2, 2, 128, 128), f32),
            pltpu.VMEM((2, NZ, 16, ROWS), f32),
            pltpu.VMEM((2, NZ, 16, ROWS), f32),
            pltpu.VMEM((2, 16, ROWS), f32),
            pltpu.VMEM((NF, 2, 128), f32),
            pltpu.VMEM((NF, 2, 128), f32),
            dma((6,)),
            dma((9,)), dma((9,)), dma((8,)), dma((8,)),
            dma((8,)), dma((8,)), dma, dma,
            dma((4,)), dma((4,)),
            dma((2, 8)), dma((2, 8)), dma, dma,
        ],
        compiler_params=pltpu.CompilerParams(collective_id=0, has_side_effects=True),
    )(
        occ, virt, ogap.reshape(1, -1), vgap.reshape(-1, 128), tiles.T, probe,
        jnp.asarray(times).reshape(NT, 1), jnp.asarray(table),
    )


def solution(mesh):
    placed = (P("pa", None), P("pa", None), P(), P(), P(), P(None, "ta"))
    return jax.shard_map(
        shards, mesh=mesh, in_specs=placed, out_specs=P("ta", None, "pa"), check_vma=False
    )
```

```python
import functools

import jax
import jax.numpy as jnp
import numpy as np
from jax import lax
from jax.experimental import pallas as pl
from jax.experimental.pallas import tpu as pltpu
from jax.sharding import PartitionSpec as P

MESH = pl.DeviceIdType.MESH
NT = 32
NVEC = 32
NF = 64
BLK = 128
NZ = 8
NX = 4
NY = 8
COLS = 16
CHIP_COLS = NY * COLS
ROWS = 256
LINK = jnp.bfloat16


def quadrature_grids(count_times, count_freqs):
    place = (np.arange(count_times) + 0.5) / count_times
    times = np.exp(np.log(0.05) + np.log(160.0) * place)
    freqs = np.exp(np.log(0.05) + np.log(400.0) * (np.arange(count_freqs) + 0.5) / count_freqs)
    table = 2.0 * times[None, :] * np.log(160.0) / count_times * np.cos(freqs[:, None] * times[None, :])
    return times.astype(np.float32), table.astype(np.float32)


def owner_block(x):
    high = jnp.where((x == 1) | (x == 2), 1, 0)
    low = jnp.where(x >= 2, 1, 0)
    return 2 * high + low


def kernel(
    occ_hbm, virt_hbm, ogap_hbm, vgap_hbm, tiles_hbm, probe_hbm, times_hbm, table_hbm, out_ref,
    ogap_ref, vgap_ref, tiles_ref, probe_ref, times_ref, table_ref,
    points, r_occ, r_virt, weights, s_occ, s_virt, polar, padded, probes, picked_out, picked_in, left,
    keep, x1_out, x1_in, x2_out, x2_in, sums, zs_out, zs_in, zs_sum, trans, arrivals,
    local_sem, y_send, y_recv, last_send, last_recv, f_send, f_recv, p_send, p_recv, ps_send, ps_recv,
    x_send, x_recv, zs_send, zs_recv, out_send, out_recv,
):
    ta = lax.axis_index("ta")
    y = lax.axis_index("pa")
    z = ta // 8
    e = ta % 8
    x = e // 2
    c = e % 2
    n_occ = occ_hbm.shape[1]
    n_virt = virt_hbm.shape[1]
    h_occ, h_virt = n_occ // 2, n_virt // 2

    def at(z_, e_, y_):
        return (z_ * 8 + e_, y_)

    barrier = pltpu.get_barrier_semaphore()
    near, far = x + 1 - 2 * lax.rem(x, 2), 3 - x
    sibling = at(z, x * 2 + 1 - c, y)
    partners = (at(z, near * 2 + c, y), at(z, far * 2 + c, y))
    greeted = [sibling, *partners]
    greeted += [at(z, e, lax.rem(y + d, NY)) for d in (1, 2, 6, 7)]
    greeted += [at(z, x * 2 + 1 - c, lax.rem(y + d, NY)) for d in (2, 6)]
    greeted += [at(lax.rem(z + d, NZ), e, y) for d in range(1, NZ)]
    for who in greeted:
        pl.semaphore_signal(barrier, inc=1, device_id=who, device_id_type=MESH)

    first = pl.multiple_of(x * 128 + z * COLS, COLS)
    mine = pl.ds(first, COLS)
    row0 = pl.multiple_of(c * ROWS, ROWS)
    own_copies = []
    for h in range(2):
        own_copies += [
            pltpu.make_async_copy(
                occ_hbm.at[mine, h * h_occ:(h + 1) * h_occ], points.at[0, h, :, :h_occ],
                local_sem.at[h]),
            pltpu.make_async_copy(
                virt_hbm.at[mine, h * h_virt:(h + 1) * h_virt], points.at[0, h, :, h_occ:],
                local_sem.at[2 + h]),
        ]
    row_copies = [
        pltpu.make_async_copy(occ_hbm.at[pl.ds(row0, ROWS), :], r_occ, local_sem.at[4]),
        pltpu.make_async_copy(virt_hbm.at[pl.ds(row0, ROWS), :], r_virt, local_sem.at[5]),
    ]
    small_copies = [
        pltpu.make_async_copy(source, target, local_sem.at[6 + i])
        for i, (source, target) in enumerate((
            (probe_hbm, probe_ref), (times_hbm, times_ref), (ogap_hbm, ogap_ref),
            (vgap_hbm, vgap_ref), (tiles_hbm, tiles_ref), (table_hbm, table_ref),
        ))
    ]
    for copy in own_copies + small_copies + row_copies:
        copy.start()
    for copy in own_copies:
        copy.wait()
    pl.semaphore_wait(barrier, len(greeted))

    sends = []

    def remote(src, dst, send, recv, who):
        copy = pltpu.make_async_remote_copy(
            src_ref=src, dst_ref=dst, send_sem=send, recv_sem=recv, device_id=who,
            device_id_type=MESH,
        )
        copy.start()
        sends.append(copy)
        return copy

    def along_y(source, target, step, sem):
        return remote(
            points.at[source, c], points.at[target, c], y_send.at[sem], y_recv.at[sem],
            at(z, e, lax.rem(y + step + NY, NY)),
        )

    def to_both(source, step, part, sem):
        y_to = lax.rem(y + step + NY, NY)
        copies = []
        for other in range(2):
            copies.append(remote(
                points.at[source, c, :, part], points.at[4, c, :, part],
                last_send.at[sem, other], last_recv.at[sem, other],
                at(z, x * 2 + lax.rem(c + other, 2), y_to),
            ))
        return copies

    gathers = {
        2: along_y(0, 2, -2, 2), 6: along_y(0, 6, 2, 6), 1: along_y(0, 1, -1, 1),
        7: along_y(0, 7, 1, 7),
    }
    for copy in small_copies:
        copy.wait()
    padded[:, :64] = probe_ref[...]
    padded[:, 64:] = jnp.zeros((NVEC, 64), jnp.bfloat16)
    probe_copies = []
    for d in range(1, 8):
        probe_copies.append(
            remote(padded, probes.at[z], p_send.at[d], p_recv.at[d],
                   at(lax.rem(z + d, NZ), e, y))
        )
    probes[z] = padded[...]

    weights[:, :n_occ] = jnp.exp(-times_ref[...] * ogap_ref[...])
    for j in range(n_virt // 128):
        weights[:, n_occ + j * 128:n_occ + (j + 1) * 128] = jnp.exp(
            -times_ref[...] * vgap_ref[j:j + 1, :]
        )

    tiles = tiles_ref[...]
    lane32 = lax.broadcasted_iota(jnp.int32, (1, 32), 1)
    lane_r = lax.broadcasted_iota(jnp.int32, (1, ROWS), 1)
    row_block = y * 4 + c * 2
    for copy in row_copies:
        copy.wait()

    def chunk(d, t_half):
        column_block = lax.rem(y + d, NY) * 4 + x
        hit = jnp.max(jnp.where(tiles == column_block, 1.0, 0.0), axis=0, keepdims=True)
        first_hit = jnp.sum(jnp.where(lane32 == row_block, hit, 0.0), axis=1, keepdims=True)
        second_hit = jnp.sum(jnp.where(lane32 == row_block + 1, hit, 0.0), axis=1, keepdims=True)
        mask = jnp.where(lane_r < BLK, first_hit, second_hit)
        for h in range(2):
            xo = points[d, h, :, :h_occ].astype(jnp.float32)
            xv = points[d, h, :, h_occ:].astype(jnp.float32)
            occ_lanes = slice(h * h_occ, (h + 1) * h_occ)
            virt_lanes = slice(h * h_virt, (h + 1) * h_virt)
            for t in range(16):
                row = t_half * 16 + t
                s_occ[t_half, t * COLS:(t + 1) * COLS, occ_lanes] = (
                    xo * weights[row:row + 1, occ_lanes]
                ).astype(jnp.bfloat16)
                s_virt[t_half, t * COLS:(t + 1) * COLS, virt_lanes] = (
                    xv * weights[row:row + 1, n_occ + h * h_virt:n_occ + (h + 1) * h_virt]
                ).astype(jnp.bfloat16)
        dims = (((1,), (1,)), ((), ()))
        green_occ = lax.dot_general(
            s_occ[t_half], r_occ[...], dims, preferred_element_type=jnp.float32
        )
        green_virt = lax.dot_general(
            s_virt[t_half], r_virt[...], dims, preferred_element_type=jnp.float32
        )
        value = (green_occ * green_virt * mask).astype(jnp.bfloat16)
        polar[t_half * 16:(t_half + 1) * 16, d * COLS:(d + 1) * COLS, :] = value.reshape(
            16, COLS, ROWS
        )

    siblings = {}

    def forward(d):
        siblings[d] = remote(
            points.at[d, c], points.at[d, c], f_send.at[d], f_recv.at[d], sibling
        )

    def both(d):
        siblings[d].wait_recv()
        chunk(d, 0)
        chunk(d, 1)

    chunk(0, 0)
    chunk(0, 1)
    quarter = (h_occ + h_virt) // 2
    gathers[2].wait_recv()
    gathers[3] = along_y(2, 3, -1, 3)
    last = to_both(2, -2, slice(0, quarter), 0)
    gathers[6].wait_recv()
    gathers[5] = along_y(6, 5, 1, 5)
    last += to_both(6, 2, slice(quarter, 2 * quarter), 1)
    for d in (2, 6):
        forward(d)
    for d in (1, 7):
        gathers[d].wait_recv()
        forward(d)
    both(1)
    for d in (3, 5):
        gathers[d].wait_recv()
        forward(d)
    both(7)
    both(2)

    for copy in probe_copies:
        copy.wait_recv()
    lane = lax.broadcasted_iota(jnp.int32, (128, CHIP_COLS), 1)
    source = lax.broadcasted_iota(jnp.int32, (128, CHIP_COLS), 0)
    matched = source == lax.rem(z, 4) * COLS + lane % COLS
    gathered = jnp.zeros((NVEC, CHIP_COLS), jnp.float32)
    for q in range(NY):
        slot = lax.rem(q - y + NY, NY)
        pick = jnp.where((lane // COLS == slot) & matched, 1.0, 0.0).astype(jnp.bfloat16)
        gathered += jnp.dot(probes[q], pick, preferred_element_type=jnp.float32)
    picked_out[...] = gathered.astype(jnp.bfloat16)
    probe_forward = remote(picked_out, picked_in, ps_send, ps_recv, sibling)
    both(6)
    both(3)
    both(5)
    probe_forward.wait_recv()
    gathered = jnp.where(
        z // 4 == c, picked_out[...].astype(jnp.float32), picked_in[...].astype(jnp.float32)
    )
    gathered = gathered.astype(jnp.bfloat16)
    orders = (
        (owner_block(3 - near), owner_block(near), owner_block(far), owner_block(x)),
        (owner_block(far + 1 - 2 * lax.rem(far, 2)), owner_block(far), owner_block(near),
         owner_block(x)),
    )
    to_row = lax.broadcasted_iota(jnp.int32, (NVEC, NVEC), 0)
    from_row = lax.broadcasted_iota(jnp.int32, (NVEC, NVEC), 1)
    for half, blocks in enumerate(orders):
        block = jnp.where(
            to_row < 16,
            jnp.where(to_row < 8, blocks[0], blocks[1]),
            jnp.where(to_row < 24, blocks[2], blocks[3]),
        )
        order = jnp.where(from_row == block * 8 + to_row % 8, 1.0, 0.0).astype(jnp.bfloat16)
        left[half] = jnp.dot(order, gathered, preferred_element_type=jnp.float32).astype(
            jnp.bfloat16
        )

    exchanges = []
    for copy in last:
        copy.wait_recv()
    for half in range(2):
        chunk(4, half)
        for t in range(16):
            terms = jnp.dot(
                left[half], polar[half * 16 + t], preferred_element_type=jnp.float32
            )
            x1_out[half, t * 16:(t + 1) * 16, :] = terms[:16].astype(LINK)
            keep[half, t] = terms[16:]
        exchanges.append(
            remote(x1_out.at[half], x1_in.at[half], x_send.at[half], x_recv.at[half],
                   partners[half])
        )
    seconds = []
    for half in range(2):
        exchanges[half].wait_recv()
        for t in range(16):
            total = keep[half, t] + x1_in[half, t * 16:(t + 1) * 16, :].astype(jnp.float32)
            x2_out[half, t * 8:(t + 1) * 8, :] = total[:8].astype(LINK)
            for side in range(2):
                sums[side, half, t * 8:(t + 1) * 8, :] = total[8:, side * 128:(side + 1) * 128]
        seconds.append(
            remote(x2_out.at[half], x2_in.at[half], x_send.at[2 + half], x_recv.at[2 + half],
                   partners[1 - half])
        )

    def along_z(half, source, target, step, sem):
        return remote(source, target, zs_send.at[half, sem], zs_recv.at[half, sem],
                      at(lax.rem(z + step + NZ, NZ), e, y))

    reduces, relays = [{}, {}], []
    for half, sign in enumerate((1, -1)):
        seconds[half].wait_recv()
        arrived = x2_in[half].astype(jnp.float32)
        for side in range(2):
            lanes = slice(side * 128, (side + 1) * 128)
            sums[side, half] += arrived[:, lanes]
            for s in range(NZ):
                zs_out[half, s, :, lanes] = sums[side, half, pl.ds(s, 16, stride=8), :]
        relays.append(
            along_z(half, zs_out.at[half, lax.rem(z + 4, NZ)], zs_in.at[half, 4], sign, 4)
        )
        for d in (5, 2, 6, 1, 7):
            reduces[half][d] = along_z(
                half, zs_out.at[half, lax.rem(z + sign * d + NZ, NZ)], zs_in.at[half, d],
                sign * d, d,
            )
    for half, sign in enumerate((1, -1)):
        relays[half].wait_recv()
        zs_sum[half] = zs_in[half, 4] + zs_out[half, lax.rem(z + sign * 3 + NZ, NZ)]
        reduces[half][3] = along_z(half, zs_sum.at[half], zs_in.at[half, 3], sign * 3, 3)
    totals = []
    for half in range(2):
        total = zs_out[half, z]
        for d in (7, 1, 6, 2, 5, 3):
            reduces[half][d].wait_recv()
            total += zs_in[half, d]
        totals.append(total)

    result = jnp.dot(
        table_ref[...], jnp.concatenate(totals, axis=0), preferred_element_type=jnp.float32,
        precision=lax.Precision.HIGHEST,
    )
    for side in range(2):
        trans[:, side, :] = result[:, side * 128:(side + 1) * 128]

    def hand_out(i, carry):
        place = i // 8
        away = jnp.where(place % 2 == 0, 4 - place // 2, 4 + (place + 1) // 2)
        to = lax.rem(z + away, NZ) * 8 + lax.rem(e + 4 + i % 8, 8)

        @pl.when(to != ta)
        def _():
            pltpu.make_async_remote_copy(
                src_ref=trans.at[to], dst_ref=arrivals.at[ta], send_sem=out_send,
                recv_sem=out_recv, device_id=(to, y), device_id_type=MESH,
            ).start()

        return carry

    lax.fori_loop(0, NF, hand_out, 0)
    arrivals[ta] = trans[ta]
    everything = pltpu.make_async_remote_copy(
        src_ref=trans.at[0:NF - 1], dst_ref=arrivals.at[0:NF - 1], send_sem=out_send,
        recv_sem=out_recv, device_id=sibling, device_id_type=MESH,
    )
    everything.wait_recv()
    for x_from in range(NX):
        block = (0, 2, 3, 1)[x_from]
        for c_from in range(2):
            for side in range(2):
                lanes = slice(c_from * ROWS + side * 128, c_from * ROWS + (side + 1) * 128)
                for z_from in range(NZ):
                    out_ref[0, block * 8 + z_from, lanes] = arrivals[
                        z_from * 8 + x_from * 2 + c_from, side
                    ]
    everything.wait_send()
    for copy in sends:
        copy.wait_send()


def shards(occ, virt, ogap, vgap, tiles, probe):
    times, table = quadrature_grids(NT, NF)
    n_occ, n_virt = occ.shape[1], virt.shape[1]
    n_all = n_occ + n_virt
    bf16, f32 = jnp.bfloat16, jnp.float32
    dma = pltpu.SemaphoreType.DMA
    vmem = pl.BlockSpec(memory_space=pltpu.VMEM)
    hbm = pl.BlockSpec(memory_space=pl.ANY)
    return pl.pallas_call(
        kernel,
        out_shape=pltpu.VMEM((1, NVEC, occ.shape[0]), f32),
        in_specs=[hbm] * 8,
        out_specs=vmem,
        scratch_shapes=[
            pltpu.VMEM((1, n_occ), f32),
            pltpu.VMEM((n_virt // 128, 128), f32),
            pltpu.VMEM(tiles.shape[::-1], jnp.int32),
            pltpu.VMEM(probe.shape, bf16),
            pltpu.VMEM((NT, 1), f32),
            pltpu.VMEM((NF, NT), f32),
            pltpu.VMEM((NY, 2, COLS, n_all // 2), bf16),
            pltpu.VMEM((ROWS, n_occ), bf16),
            pltpu.VMEM((ROWS, n_virt), bf16),
            pltpu.VMEM((NT, n_all), f32),
            pltpu.VMEM((2, 16 * COLS, n_occ), bf16),
            pltpu.VMEM((2, 16 * COLS, n_virt), bf16),
            pltpu.VMEM((NT, CHIP_COLS, ROWS), bf16),
            pltpu.VMEM((NVEC, 128), bf16),
            pltpu.VMEM((NZ, NVEC, 128), bf16),
            pltpu.VMEM((NVEC, CHIP_COLS), bf16),
            pltpu.VMEM((NVEC, CHIP_COLS), bf16),
            pltpu.VMEM((2, NVEC, CHIP_COLS), bf16),
            pltpu.VMEM((2, 16, 16, ROWS), f32),
            pltpu.VMEM((2, 256, ROWS), LINK),
            pltpu.VMEM((2, 256, ROWS), LINK),
            pltpu.VMEM((2, 128, ROWS), LINK),
            pltpu.VMEM((2, 128, ROWS), LINK),
            pltpu.VMEM((2, 2, 128, 128), f32),
            pltpu.VMEM((2, NZ, 16, ROWS), f32),
            pltpu.VMEM((2, NZ, 16, ROWS), f32),
            pltpu.VMEM((2, 16, ROWS), f32),
            pltpu.VMEM((NF, 2, 128), f32),
            pltpu.VMEM((NF, 2, 128), f32),
            dma((12,)),
            dma((8,)), dma((8,)), dma((2, 2)), dma((2, 2)), dma((8,)), dma((8,)),
            dma((8,)), dma((8,)), dma, dma,
            dma((4,)), dma((4,)),
            dma((2, 8)), dma((2, 8)), dma, dma,
        ],
        compiler_params=pltpu.CompilerParams(collective_id=0, has_side_effects=True),
    )(
        occ, virt, ogap.reshape(1, -1), vgap.reshape(-1, 128), tiles.T, probe,
        jnp.asarray(times).reshape(NT, 1), jnp.asarray(table),
    )


def solution(mesh):
    placed = (P("pa", None), P("pa", None), P(), P(), P(), P(None, "ta"))
    return jax.shard_map(
        shards, mesh=mesh, in_specs=placed, out_specs=P("ta", None, "pa"), check_vma=False
    )
```

```python
import itertools

import jax
import jax.numpy as jnp
import numpy as np
from jax import lax
from jax.experimental import pallas as pl
from jax.experimental.pallas import tpu as pltpu
from jax.sharding import PartitionSpec as P

MESH = pl.DeviceIdType.MESH
NT = 32
NVEC = 32
NF = 64
BLK = 128
NZ = 8
NX = 4
NY = 8
COLS = 16
CHIP_COLS = NY * COLS
ROWS = 256
LINK = jnp.bfloat16


def quadrature_grids(count_times, count_freqs):
    place = (np.arange(count_times) + 0.5) / count_times
    times = np.exp(np.log(0.05) + np.log(160.0) * place)
    freqs = np.exp(np.log(0.05) + np.log(400.0) * (np.arange(count_freqs) + 0.5) / count_freqs)
    table = 2.0 * times[None, :] * np.log(160.0) / count_times * np.cos(freqs[:, None] * times[None, :])
    return times.astype(np.float32), table.astype(np.float32)


def owner_block(x):
    high = jnp.where((x == 1) | (x == 2), 1, 0)
    low = jnp.where(x >= 2, 1, 0)
    return 2 * high + low


def kernel(
    occ_hbm, virt_hbm, ogap_hbm, vgap_hbm, tiles_hbm, probe_hbm, times_hbm, table_hbm, out_ref,
    ogap_ref, vgap_ref, tiles_ref, probe_ref, times_ref, table_ref,
    points, r_occ, r_virt, weights, s_occ, s_virt, polar, padded, probes, picked_out, picked_in, left,
    keep, x1_out, x1_in, x2_out, x2_in, sums, zs_out, zs_in, zs_sum, trans, arrivals,
    local_sem, y_send, y_recv, last_send, last_recv, f_send, f_recv, p_send, p_recv, ps_send, ps_recv,
    x_send, x_recv, zs_send, zs_recv, out_send, out_recv,
):
    ta = lax.axis_index("ta")
    y = lax.axis_index("pa")
    z = ta // 8
    e = ta % 8
    x = e // 2
    c = e % 2
    n_occ = occ_hbm.shape[1]
    n_virt = virt_hbm.shape[1]
    h_occ, h_virt = n_occ // 2, n_virt // 2

    def at(z_, e_, y_):
        return (z_ * 8 + e_, y_)

    barrier = pltpu.get_barrier_semaphore()
    near, far = x + 1 - 2 * lax.rem(x, 2), 3 - x
    sibling = at(z, x * 2 + 1 - c, y)
    partners = (at(z, near * 2 + c, y), at(z, far * 2 + c, y))
    greeted = [sibling, *partners]
    greeted += [at(z, e, lax.rem(y + d, NY)) for d in (1, 2, 6, 7)]
    greeted += [at(z, x * 2 + 1 - c, lax.rem(y + d, NY)) for d in (2, 6)]
    greeted += [at(lax.rem(z + d, NZ), e, y) for d in range(1, NZ)]
    for who in greeted:
        pl.semaphore_signal(barrier, inc=1, device_id=who, device_id_type=MESH)

    first = pl.multiple_of(x * 128 + z * COLS, COLS)
    mine = pl.ds(first, COLS)
    row0 = pl.multiple_of(c * ROWS, ROWS)
    own_copies = []
    for h in range(2):
        own_copies += [
            pltpu.make_async_copy(
                occ_hbm.at[mine, h * h_occ:(h + 1) * h_occ], points.at[0, h, :, :h_occ],
                local_sem.at[h]),
            pltpu.make_async_copy(
                virt_hbm.at[mine, h * h_virt:(h + 1) * h_virt], points.at[0, h, :, h_occ:],
                local_sem.at[2 + h]),
        ]
    row_copies = [
        pltpu.make_async_copy(occ_hbm.at[pl.ds(row0, ROWS), :], r_occ, local_sem.at[4]),
        pltpu.make_async_copy(virt_hbm.at[pl.ds(row0, ROWS), :], r_virt, local_sem.at[5]),
    ]
    small_copies = [
        pltpu.make_async_copy(source, target, local_sem.at[6 + i])
        for i, (source, target) in enumerate((
            (probe_hbm, probe_ref), (times_hbm, times_ref), (ogap_hbm, ogap_ref),
            (vgap_hbm, vgap_ref), (tiles_hbm, tiles_ref), (table_hbm, table_ref),
        ))
    ]
    for copy in own_copies + small_copies + row_copies:
        copy.start()
    for copy in own_copies:
        copy.wait()
    pl.semaphore_wait(barrier, len(greeted))

    sends = []

    def remote(src, dst, send, recv, who):
        copy = pltpu.make_async_remote_copy(
            src_ref=src, dst_ref=dst, send_sem=send, recv_sem=recv, device_id=who,
            device_id_type=MESH,
        )
        copy.start()
        sends.append(copy)
        return copy

    def along_y(source, target, step, sem, part=c):
        return remote(
            points.at[source, part], points.at[target, part], y_send.at[sem], y_recv.at[sem],
            at(z, e, lax.rem(y + step + NY, NY)),
        )

    def to_both(source, step, part, sem):
        y_to = lax.rem(y + step + NY, NY)
        copies = []
        for other in range(2):
            copies.append(remote(
                points.at[source, c, :, part], points.at[4, c, :, part],
                last_send.at[sem, other], last_recv.at[sem, other],
                at(z, x * 2 + lax.rem(c + other, 2), y_to),
            ))
        return copies

    gathers = {
        2: along_y(0, 2, -2, 2), 6: along_y(0, 6, 2, 6),
        1: along_y(0, 1, -1, 1, pl.ds(0, 2)), 7: along_y(0, 7, 1, 7, pl.ds(0, 2)),
    }
    for copy in small_copies:
        copy.wait()
    padded[:, :64] = probe_ref[...]
    padded[:, 64:] = jnp.zeros((NVEC, 64), jnp.bfloat16)
    probe_copies = []
    for d in range(1, 8):
        probe_copies.append(
            remote(padded, probes.at[z], p_send.at[d], p_recv.at[d],
                   at(lax.rem(z + d, NZ), e, y))
        )
    probes[z] = padded[...]

    weights[:, :n_occ] = jnp.exp(-times_ref[...] * ogap_ref[...])
    for j in range(n_virt // 128):
        weights[:, n_occ + j * 128:n_occ + (j + 1) * 128] = jnp.exp(
            -times_ref[...] * vgap_ref[j:j + 1, :]
        )

    tiles = tiles_ref[...]
    lane32 = lax.broadcasted_iota(jnp.int32, (1, 32), 1)
    lane_r = lax.broadcasted_iota(jnp.int32, (1, ROWS), 1)
    row_block = y * 4 + c * 2
    for copy in row_copies:
        copy.wait()

    turns = itertools.cycle(range(2))

    def chunk(d, t_half):
        turn = next(turns)
        column_block = lax.rem(y + d, NY) * 4 + x
        hit = jnp.max(jnp.where(tiles == column_block, 1.0, 0.0), axis=0, keepdims=True)
        first_hit = jnp.sum(jnp.where(lane32 == row_block, hit, 0.0), axis=1, keepdims=True)
        second_hit = jnp.sum(jnp.where(lane32 == row_block + 1, hit, 0.0), axis=1, keepdims=True)
        mask = jnp.where(lane_r < BLK, first_hit, second_hit)
        for h in range(2):
            xo = points[d, h, :, :h_occ].astype(jnp.float32)
            xv = points[d, h, :, h_occ:].astype(jnp.float32)
            occ_lanes = slice(h * h_occ, (h + 1) * h_occ)
            virt_lanes = slice(h * h_virt, (h + 1) * h_virt)
            for t in range(16):
                row = t_half * 16 + t
                s_occ[turn, t * COLS:(t + 1) * COLS, occ_lanes] = (
                    xo * weights[row:row + 1, occ_lanes]
                ).astype(jnp.bfloat16)
                s_virt[turn, t * COLS:(t + 1) * COLS, virt_lanes] = (
                    xv * weights[row:row + 1, n_occ + h * h_virt:n_occ + (h + 1) * h_virt]
                ).astype(jnp.bfloat16)
        dims = (((1,), (1,)), ((), ()))
        green_occ = lax.dot_general(
            s_occ[turn], r_occ[...], dims, preferred_element_type=jnp.float32
        )
        green_virt = lax.dot_general(
            s_virt[turn], r_virt[...], dims, preferred_element_type=jnp.float32
        )
        value = (green_occ * green_virt * mask).astype(jnp.bfloat16)
        polar[t_half * 16:(t_half + 1) * 16, d * COLS:(d + 1) * COLS, :] = value.reshape(
            16, COLS, ROWS
        )

    siblings = {}

    def forward(d):
        siblings[d] = remote(
            points.at[d, c], points.at[d, c], f_send.at[d], f_recv.at[d], sibling
        )

    chunk(0, 0)
    chunk(0, 1)
    quarter = (h_occ + h_virt) // 2
    gathers[2].wait_recv()
    gathers[3] = along_y(2, 3, -1, 3)
    last = to_both(2, -2, slice(0, quarter), 0)
    gathers[6].wait_recv()
    gathers[5] = along_y(6, 5, 1, 5)
    last += to_both(6, 2, slice(quarter, 2 * quarter), 1)
    for d in (2, 6):
        forward(d)
    for d in (1, 7):
        gathers[d].wait_recv()
        chunk(d, 0)
        chunk(d, 1)
    for d in (3, 5):
        gathers[d].wait_recv()
        forward(d)
    for d in (2, 6):
        siblings[d].wait_recv()
        chunk(d, 0)

    for copy in probe_copies:
        copy.wait_recv()
    lane = lax.broadcasted_iota(jnp.int32, (128, CHIP_COLS), 1)
    source = lax.broadcasted_iota(jnp.int32, (128, CHIP_COLS), 0)
    matched = source == lax.rem(z, 4) * COLS + lane % COLS
    gathered = jnp.zeros((NVEC, CHIP_COLS), jnp.float32)
    for q in range(NY):
        slot = lax.rem(q - y + NY, NY)
        pick = jnp.where((lane // COLS == slot) & matched, 1.0, 0.0).astype(jnp.bfloat16)
        gathered += jnp.dot(probes[q], pick, preferred_element_type=jnp.float32)
    picked_out[...] = gathered.astype(jnp.bfloat16)
    probe_forward = remote(picked_out, picked_in, ps_send, ps_recv, sibling)
    for d in (3, 5):
        siblings[d].wait_recv()
        chunk(d, 0)
    probe_forward.wait_recv()
    gathered = jnp.where(
        z // 4 == c, picked_out[...].astype(jnp.float32), picked_in[...].astype(jnp.float32)
    )
    gathered = gathered.astype(jnp.bfloat16)
    orders = (
        (owner_block(3 - near), owner_block(near), owner_block(far), owner_block(x)),
        (owner_block(far + 1 - 2 * lax.rem(far, 2)), owner_block(far), owner_block(near),
         owner_block(x)),
    )
    to_row = lax.broadcasted_iota(jnp.int32, (NVEC, NVEC), 0)
    from_row = lax.broadcasted_iota(jnp.int32, (NVEC, NVEC), 1)
    for half, blocks in enumerate(orders):
        block = jnp.where(
            to_row < 16,
            jnp.where(to_row < 8, blocks[0], blocks[1]),
            jnp.where(to_row < 24, blocks[2], blocks[3]),
        )
        order = jnp.where(from_row == block * 8 + to_row % 8, 1.0, 0.0).astype(jnp.bfloat16)
        left[half] = jnp.dot(order, gathered, preferred_element_type=jnp.float32).astype(
            jnp.bfloat16
        )

    for copy in last:
        copy.wait_recv()
    chunk(4, 0)

    exchanges = []

    def first_exchange(part):
        for i in range(8):
            terms = jnp.dot(
                left[part % 2], polar[part * 8 + i], preferred_element_type=jnp.float32
            )
            x1_out[part, i * 16:(i + 1) * 16, :] = terms[:16].astype(LINK)
            keep[part, i] = terms[16:]
        exchanges.append(
            remote(x1_out.at[part], x1_in.at[part], x_send.at[part], x_recv.at[part],
                   partners[part % 2])
        )

    seconds = []

    def second_exchange(part):
        exchanges[part].wait_recv()
        for i in range(8):
            total = keep[part, i] + x1_in[part, i * 16:(i + 1) * 16, :].astype(jnp.float32)
            x2_out[part, i * 8:(i + 1) * 8, :] = total[:8].astype(LINK)
            for side in range(2):
                sums[side, part, i * 8:(i + 1) * 8, :] = total[8:, side * 128:(side + 1) * 128]
        seconds.append(
            remote(x2_out.at[part], x2_in.at[part], x_send.at[4 + part], x_recv.at[4 + part],
                   partners[1 - part % 2])
        )

    def along_z(part, source, target, step, sem):
        return remote(source, target, zs_send.at[part, sem], zs_recv.at[part, sem],
                      at(lax.rem(z + step + NZ, NZ), e, y))

    reduces, relays = [{} for _ in range(4)], []

    def start_z(part):
        sign = 1 - 2 * (part % 2)
        seconds[part].wait_recv()
        arrived = x2_in[part].astype(jnp.float32)
        for side in range(2):
            lanes = slice(side * 128, (side + 1) * 128)
            sums[side, part] += arrived[:, lanes]
            for s in range(NZ):
                zs_out[part, s, :, lanes] = sums[side, part, pl.ds(s, 8, stride=8), :]
        relays.append(
            along_z(part, zs_out.at[part, lax.rem(z + 4, NZ)], zs_in.at[part, 4], sign, 4)
        )
        for d in (5, 2, 6, 1, 7):
            reduces[part][d] = along_z(
                part, zs_out.at[part, lax.rem(z + sign * d + NZ, NZ)], zs_in.at[part, d],
                sign * d, d,
            )

    def relay_z(part):
        sign = 1 - 2 * (part % 2)
        relays[part].wait_recv()
        zs_sum[part] = zs_in[part, 4] + zs_out[part, lax.rem(z + sign * 3 + NZ, NZ)]
        reduces[part][3] = along_z(part, zs_sum.at[part], zs_in.at[part, 3], sign * 3, 3)

    first_exchange(0)
    first_exchange(1)
    for d in (2, 6, 3, 5, 4):
        chunk(d, 1)
    first_exchange(2)
    first_exchange(3)
    second_exchange(0)
    second_exchange(1)
    second_exchange(2)
    second_exchange(3)
    start_z(0)
    start_z(1)
    start_z(2)
    relay_z(0)
    start_z(3)
    relay_z(1)
    relay_z(2)
    relay_z(3)
    totals = []
    for part in range(4):
        total = zs_out[part, z]
        for d in (7, 1, 6, 2, 5, 3):
            reduces[part][d].wait_recv()
            total += zs_in[part, d]
        totals.append(total)

    result = jnp.dot(
        table_ref[...], jnp.concatenate(totals, axis=0), preferred_element_type=jnp.float32,
        precision=lax.Precision.HIGHEST,
    )
    for side in range(2):
        trans[:, side, :] = result[:, side * 128:(side + 1) * 128]

    def hand_out(i, carry):
        place = i // 8
        away = jnp.where(place % 2 == 0, 4 - place // 2, 4 + (place + 1) // 2)
        to = lax.rem(z + away, NZ) * 8 + lax.rem(e + 4 + i % 8, 8)

        @pl.when(to != ta)
        def _():
            pltpu.make_async_remote_copy(
                src_ref=trans.at[to], dst_ref=arrivals.at[ta], send_sem=out_send,
                recv_sem=out_recv, device_id=(to, y), device_id_type=MESH,
            ).start()

        return carry

    lax.fori_loop(0, NF, hand_out, 0)
    arrivals[ta] = trans[ta]
    everything = pltpu.make_async_remote_copy(
        src_ref=trans.at[0:NF - 1], dst_ref=arrivals.at[0:NF - 1], send_sem=out_send,
        recv_sem=out_recv, device_id=sibling, device_id_type=MESH,
    )
    everything.wait_recv()
    for x_from in range(NX):
        block = (0, 2, 3, 1)[x_from]
        for c_from in range(2):
            for side in range(2):
                lanes = slice(c_from * ROWS + side * 128, c_from * ROWS + (side + 1) * 128)
                for z_from in range(NZ):
                    out_ref[0, block * 8 + z_from, lanes] = arrivals[
                        z_from * 8 + x_from * 2 + c_from, side
                    ]
    everything.wait_send()
    for copy in sends:
        copy.wait_send()


def shards(occ, virt, ogap, vgap, tiles, probe):
    times, table = quadrature_grids(NT, NF)
    n_occ, n_virt = occ.shape[1], virt.shape[1]
    n_all = n_occ + n_virt
    bf16, f32 = jnp.bfloat16, jnp.float32
    dma = pltpu.SemaphoreType.DMA
    vmem = pl.BlockSpec(memory_space=pltpu.VMEM)
    hbm = pl.BlockSpec(memory_space=pl.ANY)
    return pl.pallas_call(
        kernel,
        out_shape=pltpu.VMEM((1, NVEC, occ.shape[0]), f32),
        in_specs=[hbm] * 8,
        out_specs=vmem,
        scratch_shapes=[
            pltpu.VMEM((1, n_occ), f32),
            pltpu.VMEM((n_virt // 128, 128), f32),
            pltpu.VMEM(tiles.shape[::-1], jnp.int32),
            pltpu.VMEM(probe.shape, bf16),
            pltpu.VMEM((NT, 1), f32),
            pltpu.VMEM((NF, NT), f32),
            pltpu.VMEM((NY, 2, COLS, n_all // 2), bf16),
            pltpu.VMEM((ROWS, n_occ), bf16),
            pltpu.VMEM((ROWS, n_virt), bf16),
            pltpu.VMEM((NT, n_all), f32),
            pltpu.VMEM((2, 16 * COLS, n_occ), bf16),
            pltpu.VMEM((2, 16 * COLS, n_virt), bf16),
            pltpu.VMEM((NT, CHIP_COLS, ROWS), bf16),
            pltpu.VMEM((NVEC, 128), bf16),
            pltpu.VMEM((NZ, NVEC, 128), bf16),
            pltpu.VMEM((NVEC, CHIP_COLS), bf16),
            pltpu.VMEM((NVEC, CHIP_COLS), bf16),
            pltpu.VMEM((2, NVEC, CHIP_COLS), bf16),
            pltpu.VMEM((4, 8, 16, ROWS), f32),
            pltpu.VMEM((4, 128, ROWS), LINK),
            pltpu.VMEM((4, 128, ROWS), LINK),
            pltpu.VMEM((4, 64, ROWS), LINK),
            pltpu.VMEM((4, 64, ROWS), LINK),
            pltpu.VMEM((2, 4, 64, 128), f32),
            pltpu.VMEM((4, NZ, 8, ROWS), f32),
            pltpu.VMEM((4, NZ, 8, ROWS), f32),
            pltpu.VMEM((4, 8, ROWS), f32),
            pltpu.VMEM((NF, 2, 128), f32),
            pltpu.VMEM((NF, 2, 128), f32),
            dma((12,)),
            dma((8,)), dma((8,)), dma((2, 2)), dma((2, 2)), dma((8,)), dma((8,)),
            dma((8,)), dma((8,)), dma, dma,
            dma((8,)), dma((8,)),
            dma((4, 8)), dma((4, 8)), dma, dma,
        ],
        compiler_params=pltpu.CompilerParams(collective_id=0, has_side_effects=True),
    )(
        occ, virt, ogap.reshape(1, -1), vgap.reshape(-1, 128), tiles.T, probe,
        jnp.asarray(times).reshape(NT, 1), jnp.asarray(table),
    )


def solution(mesh):
    placed = (P("pa", None), P("pa", None), P(), P(), P(), P(None, "ta"))
    return jax.shard_map(
        shards, mesh=mesh, in_specs=placed, out_specs=P("ta", None, "pa"), check_vma=False
    )
```

```python
import itertools

import jax
import jax.numpy as jnp
import numpy as np
from jax import lax
from jax.experimental import pallas as pl
from jax.experimental.pallas import tpu as pltpu
from jax.sharding import PartitionSpec as P

MESH = pl.DeviceIdType.MESH
NT = 32
NVEC = 32
NF = 64
BLK = 128
NZ = 8
NX = 4
NY = 8
COLS = 16
CHIP_COLS = NY * COLS
ROWS = 256
LINK = jnp.bfloat16


def quadrature_grids(count_times, count_freqs):
    place = (np.arange(count_times) + 0.5) / count_times
    times = np.exp(np.log(0.05) + np.log(160.0) * place)
    freqs = np.exp(np.log(0.05) + np.log(400.0) * (np.arange(count_freqs) + 0.5) / count_freqs)
    table = 2.0 * times[None, :] * np.log(160.0) / count_times * np.cos(freqs[:, None] * times[None, :])
    return times.astype(np.float32), table.astype(np.float32)


def owner_block(x):
    high = jnp.where((x == 1) | (x == 2), 1, 0)
    low = jnp.where(x >= 2, 1, 0)
    return 2 * high + low


def kernel(
    occ_hbm, virt_hbm, ogap_hbm, vgap_hbm, tiles_hbm, probe_hbm, times_hbm, table_hbm, out_ref,
    ogap_ref, vgap_ref, tiles_ref, probe_ref, times_ref, table_ref,
    points, r_occ, r_virt, weights, s_occ, s_virt, polar, padded, probes, picked_out, picked_in, left,
    keep, x1_out, x1_in, x2_out, x2_in, sums, zs_out, zs_in, zs_sum, trans, arrivals,
    local_sem, y_send, y_recv, last_send, last_recv, f_send, f_recv, p_send, p_recv, ps_send, ps_recv,
    x_send, x_recv, zs_send, zs_recv, out_send, out_recv,
):
    ta = lax.axis_index("ta")
    y = lax.axis_index("pa")
    z = ta // 8
    e = ta % 8
    x = e // 2
    c = e % 2
    n_occ = occ_hbm.shape[1]
    n_virt = virt_hbm.shape[1]
    h_occ, h_virt = n_occ // 2, n_virt // 2

    def at(z_, e_, y_):
        return (z_ * 8 + e_, y_)

    barrier = pltpu.get_barrier_semaphore()
    near, far = x + 1 - 2 * lax.rem(x, 2), 3 - x
    sibling = at(z, x * 2 + 1 - c, y)
    partners = (at(z, near * 2 + c, y), at(z, far * 2 + c, y))
    greeted = [sibling, *partners]
    greeted += [at(z, e, lax.rem(y + d, NY)) for d in (1, 2, 6, 7)]
    greeted += [at(z, x * 2 + 1 - c, lax.rem(y + d, NY)) for d in (2, 6)]
    greeted += [at(lax.rem(z + d, NZ), e, y) for d in range(1, NZ)]
    for who in greeted:
        pl.semaphore_signal(barrier, inc=1, device_id=who, device_id_type=MESH)

    first = pl.multiple_of(x * 128 + z * COLS, COLS)
    mine = pl.ds(first, COLS)
    row0 = pl.multiple_of(c * ROWS, ROWS)
    own_copies = []
    for h in range(2):
        own_copies += [
            pltpu.make_async_copy(
                occ_hbm.at[mine, h * h_occ:(h + 1) * h_occ], points.at[0, h, :, :h_occ],
                local_sem.at[h]),
            pltpu.make_async_copy(
                virt_hbm.at[mine, h * h_virt:(h + 1) * h_virt], points.at[0, h, :, h_occ:],
                local_sem.at[2 + h]),
        ]
    row_copies = [
        pltpu.make_async_copy(occ_hbm.at[pl.ds(row0, ROWS), :], r_occ, local_sem.at[4]),
        pltpu.make_async_copy(virt_hbm.at[pl.ds(row0, ROWS), :], r_virt, local_sem.at[5]),
    ]
    small_copies = [
        pltpu.make_async_copy(source, target, local_sem.at[6 + i])
        for i, (source, target) in enumerate((
            (probe_hbm, probe_ref), (times_hbm, times_ref), (ogap_hbm, ogap_ref),
            (vgap_hbm, vgap_ref), (tiles_hbm, tiles_ref), (table_hbm, table_ref),
        ))
    ]
    for copy in own_copies + small_copies + row_copies:
        copy.start()
    for copy in own_copies:
        copy.wait()
    pl.semaphore_wait(barrier, len(greeted))

    sends = []

    def remote(src, dst, send, recv, who):
        copy = pltpu.make_async_remote_copy(
            src_ref=src, dst_ref=dst, send_sem=send, recv_sem=recv, device_id=who,
            device_id_type=MESH,
        )
        copy.start()
        sends.append(copy)
        return copy

    def along_y(source, target, step, sem):
        return remote(
            points.at[source, c], points.at[target, c], y_send.at[sem], y_recv.at[sem],
            at(z, e, lax.rem(y + step + NY, NY)),
        )

    def to_both(source, step, part, sem):
        y_to = lax.rem(y + step + NY, NY)
        copies = []
        for other in range(2):
            copies.append(remote(
                points.at[source, c, :, part], points.at[4, c, :, part],
                last_send.at[sem, other], last_recv.at[sem, other],
                at(z, x * 2 + lax.rem(c + other, 2), y_to),
            ))
        return copies

    gathers = {
        2: along_y(0, 2, -2, 2), 6: along_y(0, 6, 2, 6),
        1: along_y(0, 1, -1, 1), 7: along_y(0, 7, 1, 7),
    }
    for copy in small_copies:
        copy.wait()
    padded[:, :64] = probe_ref[...]
    padded[:, 64:] = jnp.zeros((NVEC, 64), jnp.bfloat16)
    probe_copies = []
    for d in range(1, 8):
        probe_copies.append(
            remote(padded, probes.at[z], p_send.at[d], p_recv.at[d],
                   at(lax.rem(z + d, NZ), e, y))
        )
    probes[z] = padded[...]

    weights[:, :n_occ] = jnp.exp(-times_ref[...] * ogap_ref[...])
    for j in range(n_virt // 128):
        weights[:, n_occ + j * 128:n_occ + (j + 1) * 128] = jnp.exp(
            -times_ref[...] * vgap_ref[j:j + 1, :]
        )

    tiles = tiles_ref[...]
    lane32 = lax.broadcasted_iota(jnp.int32, (1, 32), 1)
    lane_r = lax.broadcasted_iota(jnp.int32, (1, ROWS), 1)
    row_block = y * 4 + c * 2
    for copy in row_copies:
        copy.wait()

    turns = itertools.cycle(range(2))

    def chunk(d, t_half):
        turn = next(turns)
        column_block = lax.rem(y + d, NY) * 4 + x
        hit = jnp.max(jnp.where(tiles == column_block, 1.0, 0.0), axis=0, keepdims=True)
        first_hit = jnp.sum(jnp.where(lane32 == row_block, hit, 0.0), axis=1, keepdims=True)
        second_hit = jnp.sum(jnp.where(lane32 == row_block + 1, hit, 0.0), axis=1, keepdims=True)
        mask = jnp.where(lane_r < BLK, first_hit, second_hit)
        for h in range(2):
            xo = points[d, h, :, :h_occ].astype(jnp.float32)
            xv = points[d, h, :, h_occ:].astype(jnp.float32)
            occ_lanes = slice(h * h_occ, (h + 1) * h_occ)
            virt_lanes = slice(h * h_virt, (h + 1) * h_virt)
            for t in range(16):
                row = t_half * 16 + t
                s_occ[turn, t * COLS:(t + 1) * COLS, occ_lanes] = (
                    xo * weights[row:row + 1, occ_lanes]
                ).astype(jnp.bfloat16)
                s_virt[turn, t * COLS:(t + 1) * COLS, virt_lanes] = (
                    xv * weights[row:row + 1, n_occ + h * h_virt:n_occ + (h + 1) * h_virt]
                ).astype(jnp.bfloat16)
        dims = (((1,), (1,)), ((), ()))
        green_occ = lax.dot_general(
            s_occ[turn], r_occ[...], dims, preferred_element_type=jnp.float32
        )
        green_virt = lax.dot_general(
            s_virt[turn], r_virt[...], dims, preferred_element_type=jnp.float32
        )
        value = (green_occ * green_virt * mask).astype(jnp.bfloat16)
        polar[t_half * 16:(t_half + 1) * 16, d * COLS:(d + 1) * COLS, :] = value.reshape(
            16, COLS, ROWS
        )

    siblings = {}

    def forward(d):
        siblings[d] = remote(
            points.at[d, c], points.at[d, c], f_send.at[d], f_recv.at[d], sibling
        )

    chunk(0, 0)
    chunk(0, 1)
    quarter = (h_occ + h_virt) // 2
    gathers[2].wait_recv()
    gathers[3] = along_y(2, 3, -1, 3)
    last = to_both(2, -2, slice(0, quarter), 0)
    gathers[6].wait_recv()
    gathers[5] = along_y(6, 5, 1, 5)
    last += to_both(6, 2, slice(quarter, 2 * quarter), 1)
    for d in (1, 7):
        gathers[d].wait_recv()
        forward(d)
    for d in (2, 6):
        forward(d)
    for d in (1, 7):
        siblings[d].wait_recv()
        chunk(d, 0)
        chunk(d, 1)
    for d in (3, 5):
        gathers[d].wait_recv()
        forward(d)
    for d in (2, 6):
        siblings[d].wait_recv()
        chunk(d, 0)

    for copy in probe_copies:
        copy.wait_recv()
    lane = lax.broadcasted_iota(jnp.int32, (128, CHIP_COLS), 1)
    source = lax.broadcasted_iota(jnp.int32, (128, CHIP_COLS), 0)
    matched = source == lax.rem(z, 4) * COLS + lane % COLS
    gathered = jnp.zeros((NVEC, CHIP_COLS), jnp.float32)
    for q in range(NY):
        slot = lax.rem(q - y + NY, NY)
        pick = jnp.where((lane // COLS == slot) & matched, 1.0, 0.0).astype(jnp.bfloat16)
        gathered += jnp.dot(probes[q], pick, preferred_element_type=jnp.float32)
    picked_out[...] = gathered.astype(jnp.bfloat16)
    probe_forward = remote(picked_out, picked_in, ps_send, ps_recv, sibling)
    for d in (3, 5):
        siblings[d].wait_recv()
        chunk(d, 0)
    probe_forward.wait_recv()
    gathered = jnp.where(
        z // 4 == c, picked_out[...].astype(jnp.float32), picked_in[...].astype(jnp.float32)
    )
    gathered = gathered.astype(jnp.bfloat16)
    orders = (
        (owner_block(3 - near), owner_block(near), owner_block(far), owner_block(x)),
        (owner_block(far + 1 - 2 * lax.rem(far, 2)), owner_block(far), owner_block(near),
         owner_block(x)),
    )
    to_row = lax.broadcasted_iota(jnp.int32, (NVEC, NVEC), 0)
    from_row = lax.broadcasted_iota(jnp.int32, (NVEC, NVEC), 1)
    for half, blocks in enumerate(orders):
        block = jnp.where(
            to_row < 16,
            jnp.where(to_row < 8, blocks[0], blocks[1]),
            jnp.where(to_row < 24, blocks[2], blocks[3]),
        )
        order = jnp.where(from_row == block * 8 + to_row % 8, 1.0, 0.0).astype(jnp.bfloat16)
        left[half] = jnp.dot(order, gathered, preferred_element_type=jnp.float32).astype(
            jnp.bfloat16
        )

    for copy in last:
        copy.wait_recv()
    chunk(4, 0)

    exchanges = []

    def first_exchange(part):
        for i in range(8):
            terms = jnp.dot(
                left[part % 2], polar[part * 8 + i], preferred_element_type=jnp.float32
            )
            x1_out[part, i * 16:(i + 1) * 16, :] = terms[:16].astype(LINK)
            keep[part, i] = terms[16:]
        exchanges.append(
            remote(x1_out.at[part], x1_in.at[part], x_send.at[part], x_recv.at[part],
                   partners[part % 2])
        )

    seconds = []

    def second_exchange(part):
        exchanges[part].wait_recv()
        for i in range(8):
            total = keep[part, i] + x1_in[part, i * 16:(i + 1) * 16, :].astype(jnp.float32)
            x2_out[part, i * 8:(i + 1) * 8, :] = total[:8].astype(LINK)
            for side in range(2):
                sums[side, part, i * 8:(i + 1) * 8, :] = total[8:, side * 128:(side + 1) * 128]
        seconds.append(
            remote(x2_out.at[part], x2_in.at[part], x_send.at[4 + part], x_recv.at[4 + part],
                   partners[1 - part % 2])
        )

    def along_z(part, source, step, sem):
        return remote(source, zs_in.at[part, sem], zs_send.at[part, sem], zs_recv.at[part, sem],
                      at(lax.rem(z + step + NZ, NZ), e, y))

    hops = [{} for _ in range(4)]

    def piece(part, distance):
        return zs_out.at[part, lax.rem(z + distance + NZ, NZ)]

    def start_z(part):
        sign = 1 - 2 * (part % 2)
        seconds[part].wait_recv()
        arrived = x2_in[part].astype(jnp.float32)
        for side in range(2):
            lanes = slice(side * 128, (side + 1) * 128)
            sums[side, part] += arrived[:, lanes]
            for s in range(NZ):
                zs_out[part, s, :, lanes] = sums[side, part, pl.ds(s, 8, stride=8), :]
        hops[part][0] = along_z(part, piece(part, 4), sign, 0)
        hops[part][4] = along_z(part, piece(part, -3 * sign), -sign, 4)

    def carry_on(part, step):
        sign = 1 - 2 * (part % 2)
        for first, sense, distance in ((0, sign, 4 - step), (4, -sign, 3 - step)):
            if distance:
                hops[part][first + step - 1].wait_recv()
                zs_sum[part, first + step] = (
                    zs_in[part, first + step - 1] + piece(part, sense * distance)[...]
                )
                hops[part][first + step] = along_z(
                    part, zs_sum.at[part, first + step], sense, first + step
                )

    first_exchange(0)
    first_exchange(1)
    for d in (2, 6, 3, 5, 4):
        chunk(d, 1)
    first_exchange(2)
    first_exchange(3)
    second_exchange(0)
    second_exchange(1)
    second_exchange(2)
    second_exchange(3)
    for part in range(4):
        start_z(part)
    for step in range(1, 4):
        for part in range(4):
            carry_on(part, step)
    totals = []
    for part in range(4):
        hops[part][3].wait_recv()
        hops[part][6].wait_recv()
        totals.append(zs_out[part, z] + zs_in[part, 3] + zs_in[part, 6])

    result = jnp.dot(
        table_ref[...], jnp.concatenate(totals, axis=0), preferred_element_type=jnp.float32,
        precision=lax.Precision.HIGHEST,
    )
    for side in range(2):
        trans[:, side, :] = result[:, side * 128:(side + 1) * 128]

    def hand_out(i, carry):
        place = i // 8
        away = jnp.where(place % 2 == 0, 4 - place // 2, 4 + (place + 1) // 2)
        to = lax.rem(z + away, NZ) * 8 + lax.rem(e + 4 + i % 8, 8)

        @pl.when(to != ta)
        def _():
            pltpu.make_async_remote_copy(
                src_ref=trans.at[to], dst_ref=arrivals.at[ta], send_sem=out_send,
                recv_sem=out_recv, device_id=(to, y), device_id_type=MESH,
            ).start()

        return carry

    lax.fori_loop(0, NF, hand_out, 0)
    arrivals[ta] = trans[ta]
    everything = pltpu.make_async_remote_copy(
        src_ref=trans.at[0:NF - 1], dst_ref=arrivals.at[0:NF - 1], send_sem=out_send,
        recv_sem=out_recv, device_id=sibling, device_id_type=MESH,
    )
    everything.wait_recv()
    for x_from in range(NX):
        block = (0, 2, 3, 1)[x_from]
        for c_from in range(2):
            for side in range(2):
                lanes = slice(c_from * ROWS + side * 128, c_from * ROWS + (side + 1) * 128)
                for z_from in range(NZ):
                    out_ref[0, block * 8 + z_from, lanes] = arrivals[
                        z_from * 8 + x_from * 2 + c_from, side
                    ]
    everything.wait_send()
    for copy in sends:
        copy.wait_send()


def shards(occ, virt, ogap, vgap, tiles, probe):
    times, table = quadrature_grids(NT, NF)
    n_occ, n_virt = occ.shape[1], virt.shape[1]
    n_all = n_occ + n_virt
    bf16, f32 = jnp.bfloat16, jnp.float32
    dma = pltpu.SemaphoreType.DMA
    vmem = pl.BlockSpec(memory_space=pltpu.VMEM)
    hbm = pl.BlockSpec(memory_space=pl.ANY)
    return pl.pallas_call(
        kernel,
        out_shape=pltpu.VMEM((1, NVEC, occ.shape[0]), f32),
        in_specs=[hbm] * 8,
        out_specs=vmem,
        scratch_shapes=[
            pltpu.VMEM((1, n_occ), f32),
            pltpu.VMEM((n_virt // 128, 128), f32),
            pltpu.VMEM(tiles.shape[::-1], jnp.int32),
            pltpu.VMEM(probe.shape, bf16),
            pltpu.VMEM((NT, 1), f32),
            pltpu.VMEM((NF, NT), f32),
            pltpu.VMEM((NY, 2, COLS, n_all // 2), bf16),
            pltpu.VMEM((ROWS, n_occ), bf16),
            pltpu.VMEM((ROWS, n_virt), bf16),
            pltpu.VMEM((NT, n_all), f32),
            pltpu.VMEM((2, 16 * COLS, n_occ), bf16),
            pltpu.VMEM((2, 16 * COLS, n_virt), bf16),
            pltpu.VMEM((NT, CHIP_COLS, ROWS), bf16),
            pltpu.VMEM((NVEC, 128), bf16),
            pltpu.VMEM((NZ, NVEC, 128), bf16),
            pltpu.VMEM((NVEC, CHIP_COLS), bf16),
            pltpu.VMEM((NVEC, CHIP_COLS), bf16),
            pltpu.VMEM((2, NVEC, CHIP_COLS), bf16),
            pltpu.VMEM((4, 8, 16, ROWS), f32),
            pltpu.VMEM((4, 128, ROWS), LINK),
            pltpu.VMEM((4, 128, ROWS), LINK),
            pltpu.VMEM((4, 64, ROWS), LINK),
            pltpu.VMEM((4, 64, ROWS), LINK),
            pltpu.VMEM((2, 4, 64, 128), f32),
            pltpu.VMEM((4, NZ, 8, ROWS), f32),
            pltpu.VMEM((4, NZ, 8, ROWS), f32),
            pltpu.VMEM((4, 8, 8, ROWS), f32),
            pltpu.VMEM((NF, 2, 128), f32),
            pltpu.VMEM((NF, 2, 128), f32),
            dma((12,)),
            dma((8,)), dma((8,)), dma((2, 2)), dma((2, 2)), dma((8,)), dma((8,)),
            dma((8,)), dma((8,)), dma, dma,
            dma((8,)), dma((8,)),
            dma((4, 8)), dma((4, 8)), dma, dma,
        ],
        compiler_params=pltpu.CompilerParams(collective_id=0, has_side_effects=True),
    )(
        occ, virt, ogap.reshape(1, -1), vgap.reshape(-1, 128), tiles.T, probe,
        jnp.asarray(times).reshape(NT, 1), jnp.asarray(table),
    )


def solution(mesh):
    placed = (P("pa", None), P("pa", None), P(), P(), P(), P(None, "ta"))
    return jax.shard_map(
        shards, mesh=mesh, in_specs=placed, out_specs=P("ta", None, "pa"), check_vma=False
    )
```

```python
import itertools

import jax
import jax.numpy as jnp
import numpy as np
from jax import lax
from jax.experimental import pallas as pl
from jax.experimental.pallas import tpu as pltpu
from jax.sharding import PartitionSpec as P

MESH = pl.DeviceIdType.MESH
NT = 32
NVEC = 32
NF = 64
Z_GROUPS = 2
BLK = 128
NZ = 8
NX = 4
NY = 8
COLS = 16
CHIP_COLS = NY * COLS
ROWS = 256
LINK = jnp.bfloat16


def quadrature_grids(count_times, count_freqs):
    place = (np.arange(count_times) + 0.5) / count_times
    times = np.exp(np.log(0.05) + np.log(160.0) * place)
    freqs = np.exp(np.log(0.05) + np.log(400.0) * (np.arange(count_freqs) + 0.5) / count_freqs)
    table = 2.0 * times[None, :] * np.log(160.0) / count_times * np.cos(freqs[:, None] * times[None, :])
    return times.astype(np.float32), table.astype(np.float32)


def owner_block(x):
    high = jnp.where((x == 1) | (x == 2), 1, 0)
    low = jnp.where(x >= 2, 1, 0)
    return 2 * high + low


def kernel(
    occ_hbm, virt_hbm, ogap_hbm, vgap_hbm, tiles_hbm, probe_hbm, times_hbm, table_hbm, out_ref,
    ogap_ref, vgap_ref, tiles_ref, probe_ref, times_ref, table_ref,
    points, r_occ, r_virt, weights, s_occ, s_virt, polar, padded, probes, picked_out, picked_in, left,
    keep, x1_out, x1_in, x2_out, x2_in, sums, zs_out, zs_in, trans, arrivals,
    local_sem, y_send, y_recv, last_send, last_recv, f_send, f_recv, p_send, p_recv, ps_send, ps_recv,
    x_send, x_recv, zs_send, zs_recv, out_send, out_recv,
):
    ta = lax.axis_index("ta")
    y = lax.axis_index("pa")
    z = ta // 8
    e = ta % 8
    x = e // 2
    c = e % 2
    n_occ = occ_hbm.shape[1]
    n_virt = virt_hbm.shape[1]
    h_occ, h_virt = n_occ // 2, n_virt // 2

    def at(z_, e_, y_):
        return (z_ * 8 + e_, y_)

    barrier = pltpu.get_barrier_semaphore()
    near, far = x + 1 - 2 * lax.rem(x, 2), 3 - x
    sibling = at(z, x * 2 + 1 - c, y)
    partners = (at(z, near * 2 + c, y), at(z, far * 2 + c, y))
    greeted = [sibling, *partners]
    greeted += [at(z, e, lax.rem(y + d, NY)) for d in (1, 2, 6, 7)]
    greeted += [at(z, x * 2 + 1 - c, lax.rem(y + d, NY)) for d in (2, 6)]
    greeted += [at(lax.rem(z + d, NZ), e, y) for d in range(1, NZ)]
    for who in greeted:
        pl.semaphore_signal(barrier, inc=1, device_id=who, device_id_type=MESH)

    first = pl.multiple_of(x * 128 + z * COLS, COLS)
    mine = pl.ds(first, COLS)
    row0 = pl.multiple_of(c * ROWS, ROWS)
    own_copies = []
    for h in range(2):
        own_copies += [
            pltpu.make_async_copy(
                occ_hbm.at[mine, h * h_occ:(h + 1) * h_occ], points.at[0, h, :, :h_occ],
                local_sem.at[h]),
            pltpu.make_async_copy(
                virt_hbm.at[mine, h * h_virt:(h + 1) * h_virt], points.at[0, h, :, h_occ:],
                local_sem.at[2 + h]),
        ]
    row_copies = [
        pltpu.make_async_copy(occ_hbm.at[pl.ds(row0, ROWS), :], r_occ, local_sem.at[4]),
        pltpu.make_async_copy(virt_hbm.at[pl.ds(row0, ROWS), :], r_virt, local_sem.at[5]),
    ]
    small_copies = [
        pltpu.make_async_copy(source, target, local_sem.at[6 + i])
        for i, (source, target) in enumerate((
            (probe_hbm, probe_ref), (times_hbm, times_ref), (ogap_hbm, ogap_ref),
            (vgap_hbm, vgap_ref), (tiles_hbm, tiles_ref), (table_hbm, table_ref),
        ))
    ]
    for copy in own_copies + small_copies + row_copies:
        copy.start()
    for copy in own_copies:
        copy.wait()
    pl.semaphore_wait(barrier, len(greeted))

    sends = []

    def remote(src, dst, send, recv, who):
        copy = pltpu.make_async_remote_copy(
            src_ref=src, dst_ref=dst, send_sem=send, recv_sem=recv, device_id=who,
            device_id_type=MESH,
        )
        copy.start()
        sends.append(copy)
        return copy

    def along_y(source, target, step, sem):
        return remote(
            points.at[source, c], points.at[target, c], y_send.at[sem], y_recv.at[sem],
            at(z, e, lax.rem(y + step + NY, NY)),
        )

    def to_both(source, step, part, sem):
        y_to = lax.rem(y + step + NY, NY)
        copies = []
        for other in range(2):
            copies.append(remote(
                points.at[source, c, :, part], points.at[4, c, :, part],
                last_send.at[sem, other], last_recv.at[sem, other],
                at(z, x * 2 + lax.rem(c + other, 2), y_to),
            ))
        return copies

    gathers = {
        2: along_y(0, 2, -2, 2), 6: along_y(0, 6, 2, 6),
        1: along_y(0, 1, -1, 1), 7: along_y(0, 7, 1, 7),
    }
    for copy in small_copies:
        copy.wait()
    padded[:, :64] = probe_ref[...]
    padded[:, 64:] = jnp.zeros((NVEC, 64), jnp.bfloat16)
    probe_copies = []
    for d in range(1, 8):
        probe_copies.append(
            remote(padded, probes.at[z], p_send.at[d], p_recv.at[d],
                   at(lax.rem(z + d, NZ), e, y))
        )
    probes[z] = padded[...]

    weights[:, :n_occ] = jnp.exp(-times_ref[...] * ogap_ref[...])
    for j in range(n_virt // 128):
        weights[:, n_occ + j * 128:n_occ + (j + 1) * 128] = jnp.exp(
            -times_ref[...] * vgap_ref[j:j + 1, :]
        )

    tiles = tiles_ref[...]
    lane32 = lax.broadcasted_iota(jnp.int32, (1, 32), 1)
    lane_r = lax.broadcasted_iota(jnp.int32, (1, ROWS), 1)
    row_block = y * 4 + c * 2
    for copy in row_copies:
        copy.wait()

    turns = itertools.cycle(range(2))

    def chunk(d, t_half):
        turn = next(turns)
        column_block = lax.rem(y + d, NY) * 4 + x
        hit = jnp.max(jnp.where(tiles == column_block, 1.0, 0.0), axis=0, keepdims=True)
        first_hit = jnp.sum(jnp.where(lane32 == row_block, hit, 0.0), axis=1, keepdims=True)
        second_hit = jnp.sum(jnp.where(lane32 == row_block + 1, hit, 0.0), axis=1, keepdims=True)
        mask = jnp.where(lane_r < BLK, first_hit, second_hit)
        for h in range(2):
            xo = points[d, h, :, :h_occ].astype(jnp.float32)
            xv = points[d, h, :, h_occ:].astype(jnp.float32)
            occ_lanes = slice(h * h_occ, (h + 1) * h_occ)
            virt_lanes = slice(h * h_virt, (h + 1) * h_virt)
            for t in range(16):
                row = t_half * 16 + t
                s_occ[turn, t * COLS:(t + 1) * COLS, occ_lanes] = (
                    xo * weights[row:row + 1, occ_lanes]
                ).astype(jnp.bfloat16)
                s_virt[turn, t * COLS:(t + 1) * COLS, virt_lanes] = (
                    xv * weights[row:row + 1, n_occ + h * h_virt:n_occ + (h + 1) * h_virt]
                ).astype(jnp.bfloat16)
        dims = (((1,), (1,)), ((), ()))
        green_occ = lax.dot_general(
            s_occ[turn], r_occ[...], dims, preferred_element_type=jnp.float32
        )
        green_virt = lax.dot_general(
            s_virt[turn], r_virt[...], dims, preferred_element_type=jnp.float32
        )
        value = (green_occ * green_virt * mask).astype(jnp.bfloat16)
        polar[t_half * 16:(t_half + 1) * 16, d * COLS:(d + 1) * COLS, :] = value.reshape(
            16, COLS, ROWS
        )

    siblings = {}

    def forward(d):
        siblings[d] = remote(
            points.at[d, c], points.at[d, c], f_send.at[d], f_recv.at[d], sibling
        )

    chunk(0, 0)
    chunk(0, 1)
    quarter = (h_occ + h_virt) // 2
    gathers[2].wait_recv()
    gathers[3] = along_y(2, 3, -1, 3)
    last = to_both(2, -2, slice(0, quarter), 0)
    gathers[6].wait_recv()
    gathers[5] = along_y(6, 5, 1, 5)
    last += to_both(6, 2, slice(quarter, 2 * quarter), 1)
    for d in (1, 7):
        gathers[d].wait_recv()
        forward(d)
    for d in (2, 6):
        forward(d)
    for d in (1, 7):
        siblings[d].wait_recv()
        chunk(d, 0)
        chunk(d, 1)
    for d in (3, 5):
        gathers[d].wait_recv()
        forward(d)
    for d in (2, 6):
        siblings[d].wait_recv()
        chunk(d, 0)

    for copy in probe_copies:
        copy.wait_recv()
    lane = lax.broadcasted_iota(jnp.int32, (128, CHIP_COLS), 1)
    source = lax.broadcasted_iota(jnp.int32, (128, CHIP_COLS), 0)
    matched = source == lax.rem(z, 4) * COLS + lane % COLS
    gathered = jnp.zeros((NVEC, CHIP_COLS), jnp.float32)
    for q in range(NY):
        slot = lax.rem(q - y + NY, NY)
        pick = jnp.where((lane // COLS == slot) & matched, 1.0, 0.0).astype(jnp.bfloat16)
        gathered += jnp.dot(probes[q], pick, preferred_element_type=jnp.float32)
    picked_out[...] = gathered.astype(jnp.bfloat16)
    probe_forward = remote(picked_out, picked_in, ps_send, ps_recv, sibling)
    for d in (3, 5):
        siblings[d].wait_recv()
        chunk(d, 0)
    probe_forward.wait_recv()
    gathered = jnp.where(
        z // 4 == c, picked_out[...].astype(jnp.float32), picked_in[...].astype(jnp.float32)
    )
    gathered = gathered.astype(jnp.bfloat16)
    orders = (
        (owner_block(3 - near), owner_block(near), owner_block(far), owner_block(x)),
        (owner_block(far + 1 - 2 * lax.rem(far, 2)), owner_block(far), owner_block(near),
         owner_block(x)),
    )
    to_row = lax.broadcasted_iota(jnp.int32, (NVEC, NVEC), 0)
    from_row = lax.broadcasted_iota(jnp.int32, (NVEC, NVEC), 1)
    for half, blocks in enumerate(orders):
        block = jnp.where(
            to_row < 16,
            jnp.where(to_row < 8, blocks[0], blocks[1]),
            jnp.where(to_row < 24, blocks[2], blocks[3]),
        )
        order = jnp.where(from_row == block * 8 + to_row % 8, 1.0, 0.0).astype(jnp.bfloat16)
        left[half] = jnp.dot(order, gathered, preferred_element_type=jnp.float32).astype(
            jnp.bfloat16
        )

    for copy in last:
        copy.wait_recv()
    chunk(4, 0)

    exchanges = []

    def first_exchange(part):
        for i in range(8):
            terms = jnp.dot(
                left[part % 2], polar[part * 8 + i], preferred_element_type=jnp.float32
            )
            x1_out[part, i * 16:(i + 1) * 16, :] = terms[:16].astype(LINK)
            keep[part, i] = terms[16:]
        exchanges.append(
            remote(x1_out.at[part], x1_in.at[part], x_send.at[part], x_recv.at[part],
                   partners[part % 2])
        )

    seconds = []

    def second_exchange(part):
        exchanges[part].wait_recv()
        for i in range(8):
            total = keep[part, i] + x1_in[part, i * 16:(i + 1) * 16, :].astype(jnp.float32)
            x2_out[part, i * 8:(i + 1) * 8, :] = total[:8].astype(LINK)
            for side in range(2):
                sums[side, part, i * 8:(i + 1) * 8, :] = total[8:, side * 128:(side + 1) * 128]
        seconds.append(
            remote(x2_out.at[part], x2_in.at[part], x_send.at[4 + part], x_recv.at[4 + part],
                   partners[1 - part % 2])
        )

    reduces = [{} for _ in range(Z_GROUPS)]

    def start_z(part):
        group, row = divmod(part * 8, NT // Z_GROUPS)
        seconds[part].wait_recv()
        arrived = x2_in[part].astype(jnp.float32)
        for side in range(2):
            lanes = slice(side * 128, (side + 1) * 128)
            sums[side, part] += arrived[:, lanes]
            for s in range(NZ):
                zs_out[group, s, row:row + 8, lanes] = sums[side, part, pl.ds(s, 8, stride=8), :]
        if row + 8 < NT // Z_GROUPS:
            return
        for d in (4, 3, 5, 2, 6, 1, 7):
            to = lax.rem(z + d, NZ)
            reduces[group][d] = remote(
                zs_out.at[group, to], zs_in.at[group, d], zs_send.at[group, d],
                zs_recv.at[group, d], at(to, e, y),
            )

    first_exchange(0)
    first_exchange(1)
    for d in (2, 6, 3, 5, 4):
        chunk(d, 1)
    first_exchange(2)
    first_exchange(3)
    second_exchange(0)
    second_exchange(1)
    start_z(0)
    second_exchange(2)
    start_z(1)
    second_exchange(3)
    start_z(2)
    start_z(3)
    totals = []
    for group in range(Z_GROUPS):
        total = zs_out[group, z]
        for d in (7, 1, 6, 2, 5, 3, 4):
            reduces[group][d].wait_recv()
            total += zs_in[group, d]
        totals.append(total)

    result = jnp.dot(
        table_ref[...], jnp.concatenate(totals, axis=0), preferred_element_type=jnp.float32,
        precision=lax.Precision.HIGHEST,
    )
    for side in range(2):
        trans[:, side, :] = result[:, side * 128:(side + 1) * 128]

    for dz in (4, 3, 5, 2, 6, 1, 7, 0):
        z_to = lax.rem(z + dz, NZ) * 8
        for de in (4, 5, 2, 3, 6, 7, 1, 0):
            if dz or de:
                to = z_to + lax.rem(e + de, 8)
                pltpu.make_async_remote_copy(
                    src_ref=trans.at[to], dst_ref=arrivals.at[ta], send_sem=out_send,
                    recv_sem=out_recv, device_id=(to, y), device_id_type=MESH,
                ).start()
    arrivals[ta] = trans[ta]
    everything = pltpu.make_async_remote_copy(
        src_ref=trans.at[0:NF - 1], dst_ref=arrivals.at[0:NF - 1], send_sem=out_send,
        recv_sem=out_recv, device_id=sibling, device_id_type=MESH,
    )
    everything.wait_recv()
    for x_from in range(NX):
        block = (0, 2, 3, 1)[x_from]
        for c_from in range(2):
            for side in range(2):
                lanes = slice(c_from * ROWS + side * 128, c_from * ROWS + (side + 1) * 128)
                for z_from in range(NZ):
                    out_ref[0, block * 8 + z_from, lanes] = arrivals[
                        z_from * 8 + x_from * 2 + c_from, side
                    ]
    everything.wait_send()
    for copy in sends:
        copy.wait_send()


def shards(occ, virt, ogap, vgap, tiles, probe):
    times, table = quadrature_grids(NT, NF)
    n_occ, n_virt = occ.shape[1], virt.shape[1]
    n_all = n_occ + n_virt
    bf16, f32 = jnp.bfloat16, jnp.float32
    dma = pltpu.SemaphoreType.DMA
    vmem = pl.BlockSpec(memory_space=pltpu.VMEM)
    hbm = pl.BlockSpec(memory_space=pl.ANY)
    return pl.pallas_call(
        kernel,
        out_shape=pltpu.VMEM((1, NVEC, occ.shape[0]), f32),
        in_specs=[hbm] * 8,
        out_specs=vmem,
        scratch_shapes=[
            pltpu.VMEM((1, n_occ), f32),
            pltpu.VMEM((n_virt // 128, 128), f32),
            pltpu.VMEM(tiles.shape[::-1], jnp.int32),
            pltpu.VMEM(probe.shape, bf16),
            pltpu.VMEM((NT, 1), f32),
            pltpu.VMEM((NF, NT), f32),
            pltpu.VMEM((NY, 2, COLS, n_all // 2), bf16),
            pltpu.VMEM((ROWS, n_occ), bf16),
            pltpu.VMEM((ROWS, n_virt), bf16),
            pltpu.VMEM((NT, n_all), f32),
            pltpu.VMEM((2, 16 * COLS, n_occ), bf16),
            pltpu.VMEM((2, 16 * COLS, n_virt), bf16),
            pltpu.VMEM((NT, CHIP_COLS, ROWS), bf16),
            pltpu.VMEM((NVEC, 128), bf16),
            pltpu.VMEM((NZ, NVEC, 128), bf16),
            pltpu.VMEM((NVEC, CHIP_COLS), bf16),
            pltpu.VMEM((NVEC, CHIP_COLS), bf16),
            pltpu.VMEM((2, NVEC, CHIP_COLS), bf16),
            pltpu.VMEM((4, 8, 16, ROWS), f32),
            pltpu.VMEM((4, 128, ROWS), LINK),
            pltpu.VMEM((4, 128, ROWS), LINK),
            pltpu.VMEM((4, 64, ROWS), LINK),
            pltpu.VMEM((4, 64, ROWS), LINK),
            pltpu.VMEM((2, 4, 64, 128), f32),
            pltpu.VMEM((Z_GROUPS, NZ, NT // Z_GROUPS, ROWS), f32),
            pltpu.VMEM((Z_GROUPS, NZ, NT // Z_GROUPS, ROWS), f32),
            pltpu.VMEM((NF, 2, 128), f32),
            pltpu.VMEM((NF, 2, 128), f32),
            dma((12,)),
            dma((8,)), dma((8,)), dma((2, 2)), dma((2, 2)), dma((8,)), dma((8,)),
            dma((8,)), dma((8,)), dma, dma,
            dma((8,)), dma((8,)),
            dma((Z_GROUPS, 8)), dma((Z_GROUPS, 8)), dma, dma,
        ],
        compiler_params=pltpu.CompilerParams(collective_id=0, has_side_effects=True),
    )(
        occ, virt, ogap.reshape(1, -1), vgap.reshape(-1, 128), tiles.T, probe,
        jnp.asarray(times).reshape(NT, 1), jnp.asarray(table),
    )


def solution(mesh):
    placed = (P("pa", None), P("pa", None), P(), P(), P(), P(None, "ta"))
    return jax.shard_map(
        shards, mesh=mesh, in_specs=placed, out_specs=P("ta", None, "pa"), check_vma=False
    )
```

```python
import itertools

import jax
import jax.numpy as jnp
import numpy as np
from jax import lax
from jax.experimental import pallas as pl
from jax.experimental.pallas import tpu as pltpu
from jax.sharding import PartitionSpec as P

MESH = pl.DeviceIdType.MESH
NT = 32
NVEC = 32
NF = 64
Z_GROUPS = 2
BLK = 128
NZ = 8
NX = 4
NY = 8
COLS = 16
CHIP_COLS = NY * COLS
ROWS = 256
LINK = jnp.bfloat16


def quadrature_grids(count_times, count_freqs):
    place = (np.arange(count_times) + 0.5) / count_times
    times = np.exp(np.log(0.05) + np.log(160.0) * place)
    freqs = np.exp(np.log(0.05) + np.log(400.0) * (np.arange(count_freqs) + 0.5) / count_freqs)
    table = 2.0 * times[None, :] * np.log(160.0) / count_times * np.cos(freqs[:, None] * times[None, :])
    return times.astype(np.float32), table.astype(np.float32)


def owner_block(x):
    high = jnp.where((x == 1) | (x == 2), 1, 0)
    low = jnp.where(x >= 2, 1, 0)
    return 2 * high + low


def kernel(
    occ_hbm, virt_hbm, ogap_hbm, vgap_hbm, tiles_hbm, probe_hbm, times_hbm, table_hbm, out_ref,
    ogap_ref, vgap_ref, tiles_ref, probe_ref, times_ref, table_ref,
    points, r_occ, r_virt, weights, s_occ, s_virt, polar, padded, probes, picked_out, picked_in, left,
    keep, x1_out, x1_in, x2_out, x2_in, sums, zs_out, zs_in, trans, arrivals,
    local_sem, y_send, y_recv, last_send, last_recv, f_send, f_recv, p_send, p_recv, ps_send, ps_recv,
    x_send, x_recv, zs_send, zs_recv, out_send, out_recv,
):
    ta = lax.axis_index("ta")
    y = lax.axis_index("pa")
    z = ta // 8
    e = ta % 8
    x = e // 2
    c = e % 2
    n_occ = occ_hbm.shape[1]
    n_virt = virt_hbm.shape[1]
    h_occ, h_virt = n_occ // 2, n_virt // 2

    def at(z_, e_, y_):
        return (z_ * 8 + e_, y_)

    barrier = pltpu.get_barrier_semaphore()
    near, far = x + 1 - 2 * lax.rem(x, 2), 3 - x
    sibling = at(z, x * 2 + 1 - c, y)
    partners = (at(z, near * 2 + c, y), at(z, far * 2 + c, y))
    greeted = [sibling, *partners]
    greeted += [at(z, e, lax.rem(y + d, NY)) for d in (1, 2, 6, 7)]
    greeted += [at(z, x * 2 + 1 - c, lax.rem(y + d, NY)) for d in (2, 6)]
    greeted += [at(lax.rem(z + d, NZ), e, y) for d in range(1, NZ)]
    for who in greeted:
        pl.semaphore_signal(barrier, inc=1, device_id=who, device_id_type=MESH)

    first = pl.multiple_of(x * 128 + z * COLS, COLS)
    mine = pl.ds(first, COLS)
    row0 = pl.multiple_of(c * ROWS, ROWS)
    own_copies = []
    for h in range(2):
        own_copies += [
            pltpu.make_async_copy(
                occ_hbm.at[mine, h * h_occ:(h + 1) * h_occ], points.at[0, h, :, :h_occ],
                local_sem.at[h]),
            pltpu.make_async_copy(
                virt_hbm.at[mine, h * h_virt:(h + 1) * h_virt], points.at[0, h, :, h_occ:],
                local_sem.at[2 + h]),
        ]
    row_copies = [
        pltpu.make_async_copy(occ_hbm.at[pl.ds(row0, ROWS), :], r_occ, local_sem.at[4]),
        pltpu.make_async_copy(virt_hbm.at[pl.ds(row0, ROWS), :], r_virt, local_sem.at[5]),
    ]
    small_copies = [
        pltpu.make_async_copy(source, target, local_sem.at[6 + i])
        for i, (source, target) in enumerate((
            (probe_hbm, probe_ref), (times_hbm, times_ref), (ogap_hbm, ogap_ref),
            (vgap_hbm, vgap_ref), (tiles_hbm, tiles_ref), (table_hbm, table_ref),
        ))
    ]
    for copy in own_copies + small_copies + row_copies:
        copy.start()
    for copy in own_copies:
        copy.wait()
    pl.semaphore_wait(barrier, len(greeted))

    sends = []

    def remote(src, dst, send, recv, who):
        copy = pltpu.make_async_remote_copy(
            src_ref=src, dst_ref=dst, send_sem=send, recv_sem=recv, device_id=who,
            device_id_type=MESH,
        )
        copy.start()
        sends.append(copy)
        return copy

    def along_y(source, target, step, sem):
        return remote(
            points.at[source, c], points.at[target, c], y_send.at[sem], y_recv.at[sem],
            at(z, e, lax.rem(y + step + NY, NY)),
        )

    def to_both(source, step, part, sem):
        y_to = lax.rem(y + step + NY, NY)
        copies = []
        for other in range(2):
            copies.append(remote(
                points.at[source, c, :, part], points.at[4, c, :, part],
                last_send.at[sem, other], last_recv.at[sem, other],
                at(z, x * 2 + lax.rem(c + other, 2), y_to),
            ))
        return copies

    gathers = {
        2: along_y(0, 2, -2, 2), 6: along_y(0, 6, 2, 6),
        1: along_y(0, 1, -1, 1), 7: along_y(0, 7, 1, 7),
    }
    for copy in small_copies:
        copy.wait()
    padded[:, :64] = probe_ref[...]
    padded[:, 64:] = jnp.zeros((NVEC, 64), jnp.bfloat16)
    probe_copies = []
    for d in range(1, 8):
        probe_copies.append(
            remote(padded, probes.at[z], p_send.at[d], p_recv.at[d],
                   at(lax.rem(z + d, NZ), e, y))
        )
    probes[z] = padded[...]

    weights[:, :n_occ] = jnp.exp(-times_ref[...] * ogap_ref[...])
    for j in range(n_virt // 128):
        weights[:, n_occ + j * 128:n_occ + (j + 1) * 128] = jnp.exp(
            -times_ref[...] * vgap_ref[j:j + 1, :]
        )

    tiles = tiles_ref[...]
    lane32 = lax.broadcasted_iota(jnp.int32, (1, 32), 1)
    lane_r = lax.broadcasted_iota(jnp.int32, (1, ROWS), 1)
    row_block = y * 4 + c * 2
    for copy in row_copies:
        copy.wait()

    turns = itertools.cycle(range(2))

    def chunk(d, t_half):
        turn = next(turns)
        column_block = lax.rem(y + d, NY) * 4 + x
        hit = jnp.max(jnp.where(tiles == column_block, 1.0, 0.0), axis=0, keepdims=True)
        first_hit = jnp.sum(jnp.where(lane32 == row_block, hit, 0.0), axis=1, keepdims=True)
        second_hit = jnp.sum(jnp.where(lane32 == row_block + 1, hit, 0.0), axis=1, keepdims=True)
        mask = jnp.where(lane_r < BLK, first_hit, second_hit)
        for h in range(2):
            xo = points[d, h, :, :h_occ].astype(jnp.float32)
            xv = points[d, h, :, h_occ:].astype(jnp.float32)
            occ_lanes = slice(h * h_occ, (h + 1) * h_occ)
            virt_lanes = slice(h * h_virt, (h + 1) * h_virt)
            for t in range(16):
                row = t_half * 16 + t
                s_occ[turn, t * COLS:(t + 1) * COLS, occ_lanes] = (
                    xo * weights[row:row + 1, occ_lanes]
                ).astype(jnp.bfloat16)
                s_virt[turn, t * COLS:(t + 1) * COLS, virt_lanes] = (
                    xv * weights[row:row + 1, n_occ + h * h_virt:n_occ + (h + 1) * h_virt]
                ).astype(jnp.bfloat16)
        dims = (((1,), (1,)), ((), ()))
        green_occ = lax.dot_general(
            s_occ[turn], r_occ[...], dims, preferred_element_type=jnp.float32
        )
        green_virt = lax.dot_general(
            s_virt[turn], r_virt[...], dims, preferred_element_type=jnp.float32
        )
        value = (green_occ * green_virt * mask).astype(jnp.bfloat16)
        polar[t_half * 16:(t_half + 1) * 16, d * COLS:(d + 1) * COLS, :] = value.reshape(
            16, COLS, ROWS
        )

    siblings = {}

    def forward(d):
        siblings[d] = remote(
            points.at[d, c], points.at[d, c], f_send.at[d], f_recv.at[d], sibling
        )

    chunk(0, 0)
    chunk(0, 1)
    quarter = (h_occ + h_virt) // 2
    gathers[2].wait_recv()
    gathers[3] = along_y(2, 3, -1, 3)
    last = to_both(2, -2, slice(0, quarter), 0)
    gathers[6].wait_recv()
    gathers[5] = along_y(6, 5, 1, 5)
    last += to_both(6, 2, slice(quarter, 2 * quarter), 1)
    for d in (1, 7):
        gathers[d].wait_recv()
        forward(d)
    for d in (2, 6):
        forward(d)
    for d in (1, 7):
        siblings[d].wait_recv()
        chunk(d, 0)
        chunk(d, 1)
    for d in (3, 5):
        gathers[d].wait_recv()
        forward(d)
    for d in (2, 6):
        siblings[d].wait_recv()
        chunk(d, 0)
        chunk(d, 1)

    for copy in probe_copies:
        copy.wait_recv()
    lane = lax.broadcasted_iota(jnp.int32, (128, CHIP_COLS), 1)
    source = lax.broadcasted_iota(jnp.int32, (128, CHIP_COLS), 0)
    matched = source == lax.rem(z, 4) * COLS + lane % COLS
    gathered = jnp.zeros((NVEC, CHIP_COLS), jnp.float32)
    for q in range(NY):
        slot = lax.rem(q - y + NY, NY)
        pick = jnp.where((lane // COLS == slot) & matched, 1.0, 0.0).astype(jnp.bfloat16)
        gathered += jnp.dot(probes[q], pick, preferred_element_type=jnp.float32)
    picked_out[...] = gathered.astype(jnp.bfloat16)
    probe_forward = remote(picked_out, picked_in, ps_send, ps_recv, sibling)
    for d in (3, 5):
        siblings[d].wait_recv()
        chunk(d, 0)
        chunk(d, 1)
    probe_forward.wait_recv()
    gathered = jnp.where(
        z // 4 == c, picked_out[...].astype(jnp.float32), picked_in[...].astype(jnp.float32)
    )
    gathered = gathered.astype(jnp.bfloat16)
    orders = (
        (owner_block(3 - near), owner_block(near), owner_block(far), owner_block(x)),
        (owner_block(far + 1 - 2 * lax.rem(far, 2)), owner_block(far), owner_block(near),
         owner_block(x)),
    )
    to_row = lax.broadcasted_iota(jnp.int32, (NVEC, NVEC), 0)
    from_row = lax.broadcasted_iota(jnp.int32, (NVEC, NVEC), 1)
    for half, blocks in enumerate(orders):
        block = jnp.where(
            to_row < 16,
            jnp.where(to_row < 8, blocks[0], blocks[1]),
            jnp.where(to_row < 24, blocks[2], blocks[3]),
        )
        order = jnp.where(from_row == block * 8 + to_row % 8, 1.0, 0.0).astype(jnp.bfloat16)
        left[half] = jnp.dot(order, gathered, preferred_element_type=jnp.float32).astype(
            jnp.bfloat16
        )

    for copy in last:
        copy.wait_recv()
    chunk(4, 0)

    exchanges = []

    def first_exchange(part):
        for i in range(8):
            terms = jnp.dot(
                left[part % 2], polar[part * 8 + i], preferred_element_type=jnp.float32
            )
            x1_out[part, i * 16:(i + 1) * 16, :] = terms[:16].astype(LINK)
            keep[part, i] = terms[16:]
        exchanges.append(
            remote(x1_out.at[part], x1_in.at[part], x_send.at[part], x_recv.at[part],
                   partners[part % 2])
        )

    seconds = []

    def second_exchange(part):
        exchanges[part].wait_recv()
        for i in range(8):
            total = keep[part, i] + x1_in[part, i * 16:(i + 1) * 16, :].astype(jnp.float32)
            x2_out[part, i * 8:(i + 1) * 8, :] = total[:8].astype(LINK)
            for side in range(2):
                sums[side, part, i * 8:(i + 1) * 8, :] = total[8:, side * 128:(side + 1) * 128]
        seconds.append(
            remote(x2_out.at[part], x2_in.at[part], x_send.at[4 + part], x_recv.at[4 + part],
                   partners[1 - part % 2])
        )

    reduces = [{} for _ in range(Z_GROUPS)]

    def start_z(part):
        group, row = divmod(part * 8, NT // Z_GROUPS)
        seconds[part].wait_recv()
        arrived = x2_in[part].astype(jnp.float32)
        for side in range(2):
            lanes = slice(side * 128, (side + 1) * 128)
            sums[side, part] += arrived[:, lanes]
            for s in range(NZ):
                zs_out[group, s, row:row + 8, lanes] = sums[side, part, pl.ds(s, 8, stride=8), :]
        if row + 8 < NT // Z_GROUPS:
            return
        for d in (4, 3, 5, 2, 6, 1, 7):
            to = lax.rem(z + d, NZ)
            reduces[group][d] = remote(
                zs_out.at[group, to], zs_in.at[group, d], zs_send.at[group, d],
                zs_recv.at[group, d], at(to, e, y),
            )

    first_exchange(0)
    first_exchange(1)
    chunk(4, 1)
    first_exchange(2)
    first_exchange(3)
    second_exchange(0)
    second_exchange(1)
    start_z(0)
    second_exchange(2)
    start_z(1)
    second_exchange(3)
    start_z(2)
    start_z(3)
    totals = []
    for group in range(Z_GROUPS):
        total = zs_out[group, z]
        for d in (7, 1, 6, 2, 5, 3, 4):
            reduces[group][d].wait_recv()
            total += zs_in[group, d]
        totals.append(total)

    result = jnp.dot(
        table_ref[...], jnp.concatenate(totals, axis=0), preferred_element_type=jnp.float32,
        precision=lax.Precision.HIGHEST,
    )
    for side in range(2):
        trans[:, side, :] = result[:, side * 128:(side + 1) * 128]

    for dz in (4, 3, 5, 2, 6, 1, 7, 0):
        z_to = lax.rem(z + dz, NZ) * 8
        for de in (4, 5, 2, 3, 6, 7, 1, 0):
            if dz or de:
                to = z_to + lax.rem(e + de, 8)
                pltpu.make_async_remote_copy(
                    src_ref=trans.at[to], dst_ref=arrivals.at[ta], send_sem=out_send,
                    recv_sem=out_recv, device_id=(to, y), device_id_type=MESH,
                ).start()
    arrivals[ta] = trans[ta]
    everything = pltpu.make_async_remote_copy(
        src_ref=trans.at[0:NF - 1], dst_ref=arrivals.at[0:NF - 1], send_sem=out_send,
        recv_sem=out_recv, device_id=sibling, device_id_type=MESH,
    )
    for copy in sends:
        copy.wait_send()
    everything.wait_recv()
    for x_from in range(NX):
        block = (0, 2, 3, 1)[x_from]
        for c_from in range(2):
            for side in range(2):
                lanes = slice(c_from * ROWS + side * 128, c_from * ROWS + (side + 1) * 128)
                for z_from in range(NZ):
                    out_ref[0, block * 8 + z_from, lanes] = arrivals[
                        z_from * 8 + x_from * 2 + c_from, side
                    ]
    everything.wait_send()


def shards(occ, virt, ogap, vgap, tiles, probe):
    times, table = quadrature_grids(NT, NF)
    n_occ, n_virt = occ.shape[1], virt.shape[1]
    n_all = n_occ + n_virt
    bf16, f32 = jnp.bfloat16, jnp.float32
    dma = pltpu.SemaphoreType.DMA
    vmem = pl.BlockSpec(memory_space=pltpu.VMEM)
    hbm = pl.BlockSpec(memory_space=pl.ANY)
    return pl.pallas_call(
        kernel,
        out_shape=pltpu.VMEM((1, NVEC, occ.shape[0]), f32),
        in_specs=[hbm] * 8,
        out_specs=vmem,
        scratch_shapes=[
            pltpu.VMEM((1, n_occ), f32),
            pltpu.VMEM((n_virt // 128, 128), f32),
            pltpu.VMEM(tiles.shape[::-1], jnp.int32),
            pltpu.VMEM(probe.shape, bf16),
            pltpu.VMEM((NT, 1), f32),
            pltpu.VMEM((NF, NT), f32),
            pltpu.VMEM((NY, 2, COLS, n_all // 2), bf16),
            pltpu.VMEM((ROWS, n_occ), bf16),
            pltpu.VMEM((ROWS, n_virt), bf16),
            pltpu.VMEM((NT, n_all), f32),
            pltpu.VMEM((2, 16 * COLS, n_occ), bf16),
            pltpu.VMEM((2, 16 * COLS, n_virt), bf16),
            pltpu.VMEM((NT, CHIP_COLS, ROWS), bf16),
            pltpu.VMEM((NVEC, 128), bf16),
            pltpu.VMEM((NZ, NVEC, 128), bf16),
            pltpu.VMEM((NVEC, CHIP_COLS), bf16),
            pltpu.VMEM((NVEC, CHIP_COLS), bf16),
            pltpu.VMEM((2, NVEC, CHIP_COLS), bf16),
            pltpu.VMEM((4, 8, 16, ROWS), f32),
            pltpu.VMEM((4, 128, ROWS), LINK),
            pltpu.VMEM((4, 128, ROWS), LINK),
            pltpu.VMEM((4, 64, ROWS), LINK),
            pltpu.VMEM((4, 64, ROWS), LINK),
            pltpu.VMEM((2, 4, 64, 128), f32),
            pltpu.VMEM((Z_GROUPS, NZ, NT // Z_GROUPS, ROWS), f32),
            pltpu.VMEM((Z_GROUPS, NZ, NT // Z_GROUPS, ROWS), f32),
            pltpu.VMEM((NF, 2, 128), f32),
            pltpu.VMEM((NF, 2, 128), f32),
            dma((12,)),
            dma((8,)), dma((8,)), dma((2, 2)), dma((2, 2)), dma((8,)), dma((8,)),
            dma((8,)), dma((8,)), dma, dma,
            dma((8,)), dma((8,)),
            dma((Z_GROUPS, 8)), dma((Z_GROUPS, 8)), dma, dma,
        ],
        compiler_params=pltpu.CompilerParams(collective_id=0, has_side_effects=True),
    )(
        occ, virt, ogap.reshape(1, -1), vgap.reshape(-1, 128), tiles.T, probe,
        jnp.asarray(times).reshape(NT, 1), jnp.asarray(table),
    )


def solution(mesh):
    placed = (P("pa", None), P("pa", None), P(), P(), P(), P(None, "ta"))
    return jax.shard_map(
        shards, mesh=mesh, in_specs=placed, out_specs=P("ta", None, "pa"), check_vma=False
    )
```
